256 devices in a mesh: band: 8 (over y, core), tm: 32 (over x, z).
Axes of the slice: x: 4, y: 4, z: 8, core: 2. Of those that a mesh axis runs over, the one named last changes fastest.
Arguments:
- tod: bfloat16 [8, 64, 262144], P('band', None, 'tm'), may hold values from -6 to 6
- filter_taps: bfloat16 [8, 64, 2049], P('band'), may hold values from -0.125 to 0.125
- det_weights: float32 [8, 64], P('band'), may hold values from -0.75 to 0.75
- owner: int32 [8, 2048, 1], P('band', 'tm'), may hold values from 0 to 31; in each aligned block of 64 rows (0 to 63, 64 to 127, ..., all dimensions but the last counted through in order) at most 8 rows name the same one
- tile_row: int32 [8, 2048], P('band', 'tm'), may hold values from 0 to 127
- block_counts: int32 [8, 32], P('band', 'tm'), may hold values from 32 to 64, as said below
- beam_rows: float32 [8, 2, 33], P('band'), may hold values from -1 to 1
- beam_cols: float32 [8, 2, 33], P('band'), may hold values from -1 to 1
- mixing: float32 [4, 8, 2], P(None, 'band'), may hold values from -1.5 to 1.5
Outputs:
- components: float32 [4, 32, 128, 128], P(None, 'tm', 'band')
The draws below stay inside these ranges and needn't reach their ends.
Inputs may be any that keep to these rules, and one draw needn't show every extreme that they name: The owner of each scan block; among the 64 scan blocks of one time shard of one band at most 8 share an owner, and in every draw some time shard sends exactly 8 to one owner. A time shard keeps its first block_counts scan blocks, the rest carry nothing; the largest value is reached in every draw.
All inputs are finite; a program needn't handle non-finite values.
Results may differ from the reference program's by a relative error of at most 0.0003.
Values may be sent and summed in bfloat16 or wider, within the bound.
A program may use at most 128 MiB of HBM per device.

```python
import math
import jax
import jax.numpy as jnp
import numpy as np
from jax import lax

DET = 64
TAPS = 2049
PIX = 128
TROWS = 128
BEAM = 33
NBEAM = 2
NCOMP = 4
BANDS = 8
BH = 16
NSAMP = 262144
NBLK = 64
NSB = 2048
CAP = 8
MAPROWS = 4096
N_TM = 32


def draw_block_counts(key, part):
    shards = NSB // NBLK
    counts_drawn = jax.random.randint(key, (BANDS, shards), NBLK // 2, NBLK + 1)
    full_spot = jax.random.randint(jax.random.fold_in(key, 7), (), 0, BANDS * shards)
    counts_flat = counts_drawn.reshape(-1).at[full_spot].set(NBLK)
    return counts_flat.reshape(BANDS, shards).astype(jnp.int32)


def set_ends(entries, rng, least, top_value):
    longest = entries.shape.index(max(entries.shape))
    spots = []
    for shift in (0, 1):
        where = [jax.random.randint(jax.random.fold_in(rng, axis), (), 0, length) for axis, length in enumerate(entries.shape)]
        where[longest] = (where[longest] + shift) % entries.shape[longest]
        spots.append(tuple(where))
    return entries.at[spots[0]].set(least).at[spots[1]].set(top_value)


def levels(key, extent, cuts, smallest, high):
    loudness, own = 1.0, jax.random.fold_in(key, 6)
    for axis_at, blocks in cuts:
        draws = jnp.exp(jax.random.uniform(jax.random.fold_in(own, axis_at), (blocks,), jnp.float32, smallest / len(cuts), high / len(cuts)))
        loudness = loudness * jnp.repeat(draws, extent[axis_at] // blocks).reshape([-1 if axis == axis_at else 1 for axis in range(len(extent))])
    return loudness


def deal_out(key, own, number, rows, amount, top, most, skew):
    ranking = jax.random.permutation(key, amount)
    heavy_load, common = load_shares(amount, rows * top, most, skew, True), load_shares(amount, rows * top, most, skew, False)
    places = jnp.arange(amount)

    def named(sizes, rotation):
        used = int((sizes > 0).sum())
        fixed = max(1, used // 4)
        shifted = fixed + (places - fixed + rotation * (used - fixed)) % max(1, amount - fixed)
        return jnp.zeros((amount,), jnp.int32).at[ranking[jnp.where(places < fixed, places, shifted)]].set(jnp.asarray(sizes, jnp.int32))

    sizes = jnp.where(number % 4 == 0, named(heavy_load, number // 4), named(common, number - number // 4 - 1))
    mixed = jax.random.permutation(jax.random.fold_in(own, 3), amount)
    source_of, sink = mixed[0:amount // 2 * 2:2], mixed[1:amount // 2 * 2:2]
    margin = jnp.minimum(sizes[source_of] - 1, most - sizes[sink]) // 2
    margin = jnp.where((source_of == ranking[0]) | (sink == ranking[0]) | (sizes[sink] == 0), 0, jnp.maximum(margin, 0))
    shifted = jax.random.randint(jax.random.fold_in(own, 4), (amount // 2,), 0, 1 << 20) % (margin + 1)
    sizes = sizes.at[source_of].add(-shifted).at[sink].add(shifted)
    items = jnp.searchsorted(jnp.cumsum(sizes), jnp.arange(rows * top), side="right").astype(jnp.int32)
    listing = items.reshape(top, rows).T
    listing = listing[jax.random.permutation(jax.random.fold_in(own, 1), rows)]
    rotation = jax.random.randint(jax.random.fold_in(own, 2), (rows, 1), 0, top)
    return jnp.take_along_axis(listing, (jnp.arange(top)[None, :] + rotation) % top, axis=1)


def load_shares(number_of, total, reach, slope, full):
    weights = [(1 << 20) // math.isqrt(rank ** slope) + 1 for rank in range(1, number_of + 1)]
    largest = reach if full else min(reach, max(-(-total // number_of), total * weights[0] // sum(weights)))
    least = 1 if total - largest >= number_of - 1 else 0
    given, spare = [largest] + [least] * (number_of - 1), total - largest - least * (number_of - 1)
    while spare > 0:
        movable = [i for i in range(1, number_of) if given[i] < largest] or [i for i in range(1, number_of) if given[i] < reach]
        mass, remaining = sum([weights[i] for i in movable]), spare
        for i in movable:
            extra = min(reach - given[i], max(1, remaining * weights[i] // mass), spare)
            given[i] = given[i] + extra
            spare = spare - extra
    return np.array(given)


def normal_values(key, extent, spread, most, cuts=(), held_as=jnp.bfloat16):
    entries = jax.random.normal(key, extent, jnp.float32) * spread
    if len(cuts) > 0:
        entries = levels(key, extent, cuts, -0.22, 0.18) * entries
    return jnp.clip(entries, min=-most, max=most).astype(held_as)


def setup_inputs(seed: int = 0) -> dict:
    keys = jax.random.split(jax.random.key(seed), 10)
    tod = normal_values(keys[0], (BANDS, DET, NSAMP), 1.0, 6.0, ((0, 8), (2, 32)))
    filter_taps = normal_values(keys[1], (BANDS, DET, TAPS), TAPS ** -0.5, 0.125, ((0, 8),))
    det_weights = normal_values(keys[2], (BANDS, DET), DET ** -0.5, 0.75, ((0, 8),), jnp.float32)
    owner_keys = jax.random.split(jax.random.fold_in(keys[3], 1), BANDS * NSB // NBLK)
    owner_turns = jax.random.permutation(jax.random.fold_in(keys[3], 3), BANDS * NSB // NBLK)
    owner = jax.vmap(lambda own, number: deal_out(jax.random.fold_in(keys[3], 2), own, number, NBLK, N_TM, 1, CAP, 2))(owner_keys, owner_turns).reshape((BANDS, NSB, 1))
    tile_row = set_ends(jax.random.randint(keys[4], (BANDS, NSB), 0, TROWS), jax.random.fold_in(keys[4], 1), 0, TROWS - 1).astype(jnp.int32)
    block_counts = draw_block_counts(jax.random.fold_in(keys[9], 71), 0)
    beam_rows = normal_values(keys[6], (BANDS, NBEAM, BEAM), BEAM ** -0.5, 1.0, ((0, 8),), jnp.float32)
    beam_cols = normal_values(keys[7], (BANDS, NBEAM, BEAM), BEAM ** -0.5, 1.0, ((0, 8),), jnp.float32)
    mixing = normal_values(keys[8], (NCOMP, BANDS, NBEAM), (2 * BANDS) ** -0.5, 1.5, ((1, 8),), jnp.float32)
    return dict(tod=tod, filter_taps=filter_taps, det_weights=det_weights, owner=owner, tile_row=tile_row, block_counts=block_counts, beam_rows=beam_rows, beam_cols=beam_cols, mixing=mixing)


def toeplitz_rows(tap_row, seg_len):
    taps = tap_row.shape[0]
    width = seg_len + taps - 1
    padded_taps = jnp.concatenate([tap_row, jnp.zeros((seg_len,), tap_row.dtype)])
    tiled = jnp.tile(padded_taps, seg_len)[: seg_len * width]
    return tiled.reshape(seg_len, width)


def filter_group(group_args):
    padded_group, tap_group = group_args
    half_len = (tap_group.shape[1] - 1) // 2
    seg_len = math.gcd(half_len, 128)
    reach_pieces = 2 * half_len // seg_len
    group_size = padded_group.shape[0]
    segments = (padded_group.shape[1] - 2 * half_len) // seg_len
    pieces = padded_group.reshape(group_size, segments + reach_pieces, seg_len)
    windows = jnp.concatenate([pieces[:, shift:shift + segments] for shift in range(reach_pieces + 1)], axis=2)
    tables = jax.vmap(lambda tap_row: toeplitz_rows(tap_row, seg_len))(tap_group)
    product = lax.dot_general(windows.astype(jnp.float32), tables.astype(jnp.float32), (((2,), (2,)), ((0,), (0,))), precision=lax.Precision.HIGHEST, preferred_element_type=jnp.float32)
    return product.reshape(group_size, segments * seg_len)


def filter_band(tod_band, tap_rows):
    half_len = (tap_rows.shape[1] - 1) // 2
    detectors = tod_band.shape[0]
    samples = tod_band.shape[1]
    group_size = math.gcd(detectors, 16)
    padded = jnp.pad(tod_band, ((0, 0), (half_len, half_len)))
    padded = padded.reshape(detectors // group_size, group_size, samples + 2 * half_len)
    grouped_taps = tap_rows.reshape(detectors // group_size, group_size, tap_rows.shape[1])
    filtered = lax.map(filter_group, (padded, grouped_taps))
    return filtered.reshape(detectors, samples)


def reference(tod, filter_taps, det_weights, owner, tile_row, block_counts, beam_rows, beam_cols, mixing):
    def one_band(band_args):
        tod_band, tap_rows, weights, owners, pixel_rows, counts, row_profile, col_profile = band_args
        filtered = filter_band(tod_band, tap_rows)
        weighted = jnp.dot(weights, filtered, precision=lax.Precision.HIGHEST, preferred_element_type=jnp.float32)
        block_vals = weighted.reshape(NSB, PIX)
        block_index = jnp.arange(NSB, dtype=jnp.int32)
        local_index = block_index % NBLK
        shard_index = block_index // NBLK
        valid_mask = (local_index < counts[shard_index]).astype(jnp.float32)
        block_vals = block_vals * valid_mask[:, None]
        target = (owners[:, 0] * TROWS + pixel_rows).astype(jnp.int32)
        sky_map = jax.ops.segment_sum(block_vals, target, num_segments=MAPROWS)
        padded = jnp.pad(sky_map, ((BH, BH), (BH, BH)))
        results = []
        for beam in range(NBEAM):
            rowed = jnp.zeros((MAPROWS, PIX + 2 * BH), jnp.float32)
            for shift in range(BEAM):
                rowed = rowed + row_profile[beam, shift] * padded[shift:shift + MAPROWS, :]
            smoothed = jnp.zeros((MAPROWS, PIX), jnp.float32)
            for shift in range(BEAM):
                smoothed = smoothed + col_profile[beam, shift] * rowed[:, shift:shift + PIX]
            results.append(smoothed)
        return jnp.stack(results)

    beamed = lax.map(one_band, (tod, filter_taps, det_weights, owner, tile_row, block_counts, beam_rows, beam_cols))
    mixed = jnp.einsum("cbk,bkrp->crp", mixing, beamed, precision=lax.Precision.HIGHEST)
    return mixed.reshape(NCOMP, N_TM, TROWS, PIX)
```

```python
import functools

import jax
import jax.numpy as jnp
from jax import lax
from jax.experimental import pallas as pl
from jax.experimental.pallas import tpu as pltpu
from jax.sharding import PartitionSpec as P

PIX = 128
CAP = 8
HALF = 1024
LAGS = 16
BEAM = 33
REACH = 16
NBEAM = 2
NCOMP = 4
CHUNK = 1024
MESH = pl.DeviceIdType.MESH
F32 = jnp.float32
BF16 = jnp.bfloat16
NT = (((1,), (1,)), ((), ()))


def iota(shape, axis):
    return lax.broadcasted_iota(jnp.int32, shape, axis)


def split(value):
    high = value.astype(BF16)
    return high, (value - high.astype(F32)).astype(BF16)


def dot(a, b):
    return jnp.dot(a, b, preferred_element_type=F32)


def dot_nt(a, b):
    return lax.dot_general(a, b, NT, preferred_element_type=F32)


def lag_table(taps, weights, table):
    det = taps.shape[1]
    eye = iota((det, det), 0) == iota((det, det), 1)
    column = jnp.sum(jnp.where(eye, weights[0:1, :], 0.0), axis=1, keepdims=True)
    flip = jnp.where(iota((PIX, PIX), 0) + iota((PIX, PIX), 1) == PIX - 1, 1.0, 0.0).astype(BF16)
    pair = 2 * PIX
    for j in range(LAGS // 2):
        both = jnp.concatenate(
            [taps[0, :, pl.ds(pair * j + PIX * e, PIX)].astype(F32) * column for e in range(2)],
            axis=0,
        )
        high, low = split(both)
        lanes = pl.ds(2 * det * j, 2 * det)
        table[0:PIX, lanes] = dot_nt(flip, high).astype(BF16)
        table[PIX : 2 * PIX, lanes] = dot_nt(flip, low).astype(BF16)
    last = taps[0, :, 2 * HALF : 2 * HALF + 1].astype(F32) * column
    last_high = last.astype(BF16).astype(F32)
    spot = iota((det, 2 * det), 1) == iota((det, 2 * det), 0) + det
    row_high = jnp.sum(jnp.where(spot, last_high, 0.0), axis=0, keepdims=True)
    row_low = jnp.sum(jnp.where(spot, last - last_high, 0.0), axis=0, keepdims=True)
    rows = iota((16, 2 * det), 0)
    rest = (LAGS - 2) * det
    table[2 * PIX : 2 * PIX + 16, 0:rest] = jnp.zeros((16, rest), BF16)
    table[2 * PIX : 2 * PIX + 16, rest : rest + 2 * det] = jnp.where(
        rows == 0, row_high, jnp.where(rows == 1, row_low, 0.0)
    ).astype(BF16)


def filter_chunk(x, table, here, before, start, block, width):
    det = x.shape[0]
    total = None
    for q in range(LAGS // 4):
        window = jnp.concatenate(
            [x[:, pl.ds(start + PIX * (4 * q + e), width)] for e in range(4)], axis=0
        )
        part = dot(table[:, 4 * det * q : 4 * det * (q + 1)], window)
        total = part if total is None else total + part
    keeps = iota((PIX, PIX), 1) <= iota((PIX, PIX), 0)
    for k in range(width // PIX):
        lanes = slice(PIX * k, PIX * (k + 1))
        lagged = total[0:PIX, lanes] + total[PIX : 2 * PIX, lanes]
        turned = pltpu.roll(lagged, 1, 1, stride=1, stride_axis=0)
        final = total[2 * PIX : 2 * PIX + 1, lanes] + total[2 * PIX + 1 : 2 * PIX + 2, lanes]
        here[pl.ds(block + k, 1), :] = jnp.sum(
            jnp.where(keeps, turned, 0.0), axis=0, keepdims=True
        )
        before[pl.ds(block + k, 1), :] = (
            jnp.sum(jnp.where(keeps, 0.0, turned), axis=0, keepdims=True) + final
        )


def band_rows(profile, out_rows, shift):
    wide = jnp.concatenate([profile, jnp.zeros((1, PIX - BEAM), F32)], axis=1)
    spread = jnp.broadcast_to(wide, (out_rows, PIX))
    turned = pltpu.roll(spread, PIX - shift, 1, stride=1, stride_axis=0)
    tap = iota((out_rows, PIX), 1) - iota((out_rows, PIX), 0) + shift
    return jnp.where((tap >= 0) & (tap < BEAM), turned, 0.0)


def kernel(
    bands,
    shards,
    side,
    tod,
    taps,
    weights,
    owner,
    tile_row,
    counts,
    beam_rows,
    beam_cols,
    mixing,
    out,
    x,
    table,
    here,
    before,
    meta_out,
    meta_in,
    vals_out,
    vals_in,
    mix_out,
    mix_in,
    wide,
    mine,
    edge,
    load_sem,
    halo_send,
    halo_recv,
    peer_send,
    peer_recv,
    band_send,
    band_recv,
    edge_send,
    edge_recv,
):
    band = lax.axis_index("band")
    shard = lax.axis_index("tm")
    depth = shards // side
    sx, sz = lax.div(shard, side), lax.rem(shard, side)
    samples = tod.shape[2]
    blocks = samples // PIX
    share = REACH
    span = bands * share
    has_left, has_right = shard > 0, shard < shards - 1
    left, right = lax.rem(shard + shards - 1, shards), lax.rem(shard + 1, shards)

    def shard_peer(i):
        return lax.rem(sx + i // side, depth) * side + lax.rem(sz + i % side, side)

    def hops(i):
        dx, dz = i // side, i % side
        return min(dx, depth - dx) + min(dz, side - dz)

    order = sorted(range(1, shards), key=lambda i: -hops(i))

    barrier = pltpu.get_barrier_semaphore()
    for i in order:
        pl.semaphore_signal(barrier, 1, device_id=(band, shard_peer(i)), device_id_type=MESH)
    for i in range(1, bands):
        pl.semaphore_signal(barrier, 1, device_id=(lax.rem(band + i, bands), shard), device_id_type=MESH)

    @pl.when((band == 0) & has_left)
    def _():
        for b in range(1, bands):
            pl.semaphore_signal(barrier, 1, device_id=(b, left), device_id_type=MESH)

    @pl.when((band == bands - 1) & has_right)
    def _():
        for b in range(bands - 1):
            pl.semaphore_signal(barrier, 1, device_id=(b, right), device_id_type=MESH)

    load = pltpu.make_async_copy(tod.at[0], x.at[:, pl.ds(HALF, samples)], load_sem)
    load.start()

    row_i, lane_i = iota((blocks, blocks), 0), iota((blocks, blocks), 1)
    diagonal = row_i == lane_i
    owner_col = owner[0]
    owner_row = jnp.sum(jnp.where(diagonal, owner_col, 0), axis=0, keepdims=True)
    same = (owner_col == owner_row) & (row_i < lane_i)
    rank_row = jnp.sum(jnp.where(same, 1, 0), axis=0, keepdims=True)
    ox, oz = owner_row // side, owner_row % side
    group = ((ox - sx + depth) % depth) * side + (oz - sz + side) % side
    slot_row = group * CAP + rank_row
    kept = iota((1, blocks), 1) < counts[0:1, 0:1]
    slots = shards * CAP
    pick = jnp.where((iota((slots, blocks), 0) == slot_row) & kept, 1.0, 0.0).astype(BF16)
    row_col = jnp.sum(jnp.where(diagonal, tile_row[0:1, :], 0), axis=1, keepdims=True)
    row_hot = jnp.where(iota((blocks, PIX), 1) == row_col, 1.0, 0.0).astype(BF16)
    meta = dot(pick, row_hot)
    meta_out[...] = meta
    meta_in[0:CAP, :] = meta[0:CAP, :]
    mix_row = iota((NCOMP * NBEAM, PIX), 0)
    mix = jnp.zeros((NCOMP * NBEAM, PIX), F32)
    for c in range(NCOMP):
        for k in range(NBEAM):
            mix = jnp.where(mix_row == c * NBEAM + k, mixing[c, 0, k], mix)
    mix_out[...] = mix
    mix_in[0] = mix

    lag_table(taps, weights, table)
    load.wait()

    def chunk_step(index, carry):
        start = pl.multiple_of(index * CHUNK, PIX)
        filter_chunk(x, table, here, before, start, index * (CHUNK // PIX), CHUNK)
        return carry

    lax.fori_loop(1, 3, chunk_step, 0)

    pl.semaphore_wait(
        barrier,
        shards
        - 1
        + bands
        - 1
        + jnp.where((band != 0) & has_right, 1, 0)
        + jnp.where((band != bands - 1) & has_left, 1, 0),
    )

    to_right = pltpu.make_async_remote_copy(
        x.at[:, pl.ds(samples, HALF)],
        x.at[:, pl.ds(0, HALF)],
        halo_send.at[0],
        halo_recv.at[0],
        device_id=(band, right),
        device_id_type=MESH,
    )
    to_left = pltpu.make_async_remote_copy(
        x.at[:, pl.ds(HALF, HALF)],
        x.at[:, pl.ds(samples + HALF, HALF)],
        halo_send.at[1],
        halo_recv.at[1],
        device_id=(band, left),
        device_id_type=MESH,
    )

    @pl.when(has_right)
    def _():
        to_right.start()

    @pl.when(has_left)
    def _():
        to_left.start()

    def to_shards(source, target, which):
        for i in order:
            pltpu.make_async_remote_copy(
                source.at[pl.ds(CAP * i, CAP)],
                target.at[pl.ds(CAP * i, CAP)],
                peer_send.at[which],
                peer_recv.at[which],
                device_id=(band, shard_peer(i)),
                device_id_type=MESH,
            ).start()

    def from_shards(ref, sem):
        part = ref.at[pl.ds(CAP, slots - CAP)]
        pltpu.make_async_copy(part, part, sem).wait()

    to_shards(meta_out, meta_in, 0)
    for i in range(1, bands):
        pltpu.make_async_remote_copy(
            mix_out,
            mix_in.at[i],
            band_send.at[0, i],
            band_recv.at[0, i],
            device_id=(lax.rem(band + i, bands), shard),
            device_id_type=MESH,
        ).start()

    lax.fori_loop(3, 7, chunk_step, 0)

    @pl.when(has_left)
    def _():
        part = x.at[:, pl.ds(0, HALF)]
        pltpu.make_async_copy(part, part, halo_recv.at[0]).wait()

    @pl.when(jnp.logical_not(has_left))
    def _():
        x[:, 0:HALF] = jnp.zeros((x.shape[0], HALF), BF16)

    @pl.when(has_right)
    def _():
        part = x.at[:, pl.ds(samples + HALF, HALF)]
        pltpu.make_async_copy(part, part, halo_recv.at[1]).wait()

    @pl.when(jnp.logical_not(has_right))
    def _():
        x[:, pl.ds(samples + HALF, HALF)] = jnp.zeros((x.shape[0], HALF), BF16)

    for index in (samples // CHUNK - 1, 0):
        filter_chunk(
            x, table, here, before, index * CHUNK, index * (CHUNK // PIX), CHUNK
        )
    filter_chunk(x, table, here, before, samples, blocks, PIX)

    block_values = here[0:blocks, :] + before[pl.ds(1, blocks), :]
    value_high, value_low = split(block_values)
    values = dot(pick, value_high) + dot(pick, value_low)
    vals_out[...] = values
    vals_in[0:CAP, :] = values[0:CAP, :]
    to_shards(vals_out, vals_in, 1)

    long = span + 2 * REACH
    row_mats = jnp.concatenate(
        [band_rows(beam_rows[0, k : k + 1, :], long, BEAM - 1) for k in range(NBEAM)],
        axis=0,
    )
    rows_high, rows_low = split(row_mats)
    from_shards(meta_in, peer_recv.at[0])
    hot = meta_in[...].astype(BF16)
    slot_high = dot_nt(rows_high, hot).astype(BF16)
    slot_low = dot_nt(rows_low, hot).astype(BF16)
    cols = [split(band_rows(beam_cols[0, k : k + 1, :], PIX, REACH)) for k in range(NBEAM)]

    from_shards(vals_in, peer_recv.at[1])
    in_high, in_low = split(vals_in[...])
    rowed = dot(slot_high, in_high) + dot(slot_high, in_low) + dot(slot_low, in_high)
    for k in range(NBEAM):
        rowed_high, rowed_low = split(rowed[long * k : long * (k + 1), :])
        col_high, col_low = cols[k]
        wide[k] = (
            dot_nt(rowed_high, col_high) + dot_nt(rowed_low, col_high) + dot_nt(rowed_high, col_low)
        )

    below = pltpu.make_async_remote_copy(
        wide.at[:, pl.ds(REACH + span, REACH), :],
        edge.at[lax.rem(bands - band, bands)],
        edge_send.at[0],
        edge_recv.at[lax.rem(bands - band, bands)],
        device_id=(0, right),
        device_id_type=MESH,
    )
    above = pltpu.make_async_remote_copy(
        wide.at[:, pl.ds(0, REACH), :],
        edge.at[bands - 1 - band],
        edge_send.at[1],
        edge_recv.at[bands - 1 - band],
        device_id=(bands - 1, left),
        device_id_type=MESH,
    )

    @pl.when(has_right)
    def _():
        below.start()

    @pl.when(has_left)
    def _():
        above.start()

    sends = []
    for i in range(1, bands):
        peer = lax.rem(band + i, bands)
        copy = pltpu.make_async_remote_copy(
            wide.at[:, pl.ds(pl.multiple_of(REACH + share * peer, REACH), share), :],
            mine.at[i],
            band_send.at[1, i],
            band_recv.at[1, i],
            device_id=(peer, shard),
            device_id_type=MESH,
        )
        copy.start()
        sends.append(copy)
    mine[0] = wide[:, pl.ds(pl.multiple_of(REACH + share * band, REACH), share), :]
    for i in range(1, bands):
        pltpu.make_async_copy(mix_in.at[i], mix_in.at[i], band_recv.at[0, i]).wait()
    for i in range(1, bands):
        pltpu.make_async_copy(mine.at[i], mine.at[i], band_recv.at[1, i]).wait()

    @pl.when(((band == 0) & has_left) | ((band == bands - 1) & has_right))
    def _():
        for i in range(bands):
            pltpu.make_async_copy(edge.at[i], edge.at[i], edge_recv.at[i]).wait()
        mine[...] += edge[...]

    for c in range(NCOMP):
        total = None
        for i in range(bands):
            for k in range(NBEAM):
                term = mix_in[i, c * NBEAM + k : c * NBEAM + k + 1, :] * mine[i, k]
                total = term if total is None else total + term
        out[c, 0] = total

    @pl.when(has_right)
    def _():
        to_right.wait_send()
        below.wait_send()

    @pl.when(has_left)
    def _():
        to_left.wait_send()
        above.wait_send()

    from_shards(meta_out, peer_send.at[0])
    from_shards(vals_out, peer_send.at[1])
    for i in range(1, bands):
        pltpu.make_async_copy(mix_out, mix_out, band_send.at[0, i]).wait()
    for copy in sends:
        copy.wait_send()


def on_device(
    tod, filter_taps, det_weights, owner, tile_row, block_counts, beam_rows, beam_cols, mixing
):
    bands, shards = lax.axis_size("band"), lax.axis_size("tm")
    side = 8 if shards >= 16 else shards // 2
    det, samples = tod.shape[1:]
    slots = shards * CAP
    long = bands * REACH + 2 * REACH
    blocks = samples // PIX
    vmem = pl.BlockSpec(memory_space=pltpu.VMEM)
    return pl.pallas_call(
        functools.partial(kernel, bands, shards, side),
        out_shape=jax.ShapeDtypeStruct((NCOMP, 1, REACH, PIX), F32),
        in_specs=[pl.BlockSpec(memory_space=pl.ANY)]
        + [vmem] * 7
        + [pl.BlockSpec(memory_space=pltpu.SMEM)],
        out_specs=vmem,
        scratch_shapes=[
            pltpu.VMEM((det, samples + 2 * HALF), BF16),
            pltpu.VMEM((2 * PIX + 16, LAGS * det), BF16),
            pltpu.VMEM((blocks + 8, PIX), F32),
            pltpu.VMEM((blocks + 8, PIX), F32),
            pltpu.VMEM((slots, PIX), F32),
            pltpu.VMEM((slots, PIX), F32),
            pltpu.VMEM((slots, PIX), F32),
            pltpu.VMEM((slots, PIX), F32),
            pltpu.VMEM((NCOMP * NBEAM, PIX), F32),
            pltpu.VMEM((bands, NCOMP * NBEAM, PIX), F32),
            pltpu.VMEM((NBEAM, long, PIX), F32),
            pltpu.VMEM((bands, NBEAM, REACH, PIX), F32),
            pltpu.VMEM((bands, NBEAM, REACH, PIX), F32),
            pltpu.SemaphoreType.DMA,
            pltpu.SemaphoreType.DMA((2,)),
            pltpu.SemaphoreType.DMA((2,)),
            pltpu.SemaphoreType.DMA((2,)),
            pltpu.SemaphoreType.DMA((2,)),
            pltpu.SemaphoreType.DMA((2, bands)),
            pltpu.SemaphoreType.DMA((2, bands)),
            pltpu.SemaphoreType.DMA((2,)),
            pltpu.SemaphoreType.DMA((bands,)),
        ],
        compiler_params=pltpu.CompilerParams(
            collective_id=0, has_side_effects=True, vmem_limit_bytes=48 * 2**20
        ),
    )(tod, filter_taps, det_weights, owner, tile_row, block_counts, beam_rows, beam_cols, mixing)


def solution(mesh):
    placed = (
        P("band", None, "tm"),
        P("band", None, None),
        P("band", None),
        P("band", "tm", None),
        P("band", "tm"),
        P("band", "tm"),
        P("band", None, None),
        P("band", None, None),
        P(None, "band", None),
    )
    return jax.shard_map(
        on_device,
        mesh=mesh,
        in_specs=placed,
        out_specs=P(None, "tm", "band", None),
        check_vma=False,
    )
```

```python
import functools

import jax
import jax.numpy as jnp
from jax import lax
from jax.experimental import pallas as pl
from jax.experimental.pallas import tpu as pltpu
from jax.sharding import PartitionSpec as P

PIX = 128
CAP = 8
HALF = 1024
LAGS = 16
BEAM = 33
REACH = 16
NBEAM = 2
NCOMP = 4
CHUNK = 1024
STEP = CHUNK // PIX
ALL = (0, 1, 2, 3)
MESH = pl.DeviceIdType.MESH
F32 = jnp.float32
BF16 = jnp.bfloat16
NT = (((1,), (1,)), ((), ()))


def iota(shape, axis):
    return lax.broadcasted_iota(jnp.int32, shape, axis)


def split(value):
    high = value.astype(BF16)
    return high, (value - high.astype(F32)).astype(BF16)


def dot(a, b):
    return jnp.dot(a, b, preferred_element_type=F32)


def dot_nt(a, b):
    return lax.dot_general(a, b, NT, preferred_element_type=F32)


def lag_table(taps, weights, table):
    det = taps.shape[1]
    eye = iota((det, det), 0) == iota((det, det), 1)
    column = jnp.sum(jnp.where(eye, weights[0:1, :], 0.0), axis=1, keepdims=True)
    flip = jnp.where(iota((PIX, PIX), 0) + iota((PIX, PIX), 1) == PIX - 1, 1.0, 0.0).astype(BF16)
    pair = 2 * PIX
    for j in range(LAGS // 2):
        both = jnp.concatenate(
            [taps[0, :, pl.ds(pair * j + PIX * e, PIX)].astype(F32) * column for e in range(2)],
            axis=0,
        )
        high, low = split(both)
        lanes = pl.ds(2 * det * j, 2 * det)
        table[0:PIX, lanes] = dot_nt(flip, high).astype(BF16)
        table[PIX : 2 * PIX, lanes] = dot_nt(flip, low).astype(BF16)
    last = taps[0, :, 2 * HALF : 2 * HALF + 1].astype(F32) * column
    last_high = last.astype(BF16).astype(F32)
    spot = iota((det, 2 * det), 1) == iota((det, 2 * det), 0) + det
    row_high = jnp.sum(jnp.where(spot, last_high, 0.0), axis=0, keepdims=True)
    row_low = jnp.sum(jnp.where(spot, last - last_high, 0.0), axis=0, keepdims=True)
    rows = iota((16, 2 * det), 0)
    rest = (LAGS - 2) * det
    table[2 * PIX : 2 * PIX + 16, 0:rest] = jnp.zeros((16, rest), BF16)
    table[2 * PIX : 2 * PIX + 16, rest : rest + 2 * det] = jnp.where(
        rows == 0, row_high, jnp.where(rows == 1, row_low, 0.0)
    ).astype(BF16)


def lagged_sums(x, table, block, parts):
    det = x.shape[0]
    total = None
    for q in parts:
        window = jnp.concatenate(
            [
                x[:, pl.ds(pl.multiple_of(PIX * block, PIX) + PIX * (4 * q + e), CHUNK)]
                for e in range(4)
            ],
            axis=0,
        )
        part = dot(table[:, 4 * det * q : 4 * det * (q + 1)], window)
        total = part if total is None else total + part
    return total


def add_diagonals(sums, here, before, block):
    keeps = iota((PIX, PIX), 1) <= iota((PIX, PIX), 0)
    prior = None
    for k in range(STEP):
        lanes = pl.ds(PIX * k, PIX)
        turned = pltpu.roll(
            sums[0:PIX, lanes] + sums[PIX : 2 * PIX, lanes], 1, 1, stride=1, stride_axis=0
        )
        final = sums[2 * PIX : 2 * PIX + 1, lanes] + sums[2 * PIX + 1 : 2 * PIX + 2, lanes]
        merged = jnp.where(keeps, 0.0 if k == 0 else prior, turned)
        done = jnp.sum(merged, axis=0, keepdims=True) + final
        if k == 0:
            before[pl.ds(block, 1), :] = done
        else:
            here[pl.ds(block + k - 1, 1), :] = done
        prior = turned
    here[pl.ds(block + STEP - 1, 1), :] = jnp.sum(
        jnp.where(keeps, prior, 0.0), axis=0, keepdims=True
    )


def band_rows(profile, out_rows, shift):
    wide = jnp.concatenate([profile, jnp.zeros((1, PIX - BEAM), F32)], axis=1)
    spread = jnp.broadcast_to(wide, (out_rows, PIX))
    turned = pltpu.roll(spread, PIX - shift, 1, stride=1, stride_axis=0)
    tap = iota((out_rows, PIX), 1) - iota((out_rows, PIX), 0) + shift
    return jnp.where((tap >= 0) & (tap < BEAM), turned, 0.0)


def kernel(
    bands,
    shards,
    side,
    tod,
    taps_hbm,
    weights_hbm,
    owner_hbm,
    tile_row_hbm,
    counts_hbm,
    beam_rows_hbm,
    beam_cols_hbm,
    mixing_hbm,
    out,
    taps,
    weights,
    owner,
    tile_row,
    counts,
    beam_rows,
    beam_cols,
    mixing,
    x,
    table,
    here,
    before,
    even,
    odd,
    overhang,
    arrived,
    meta_out,
    meta_in,
    vals_out,
    vals_in,
    mix_out,
    mix_in,
    wide,
    mine,
    edge,
    load_sem,
    small_sem,
    halo_send,
    halo_recv,
    peer_send,
    peer_recv,
    band_send,
    band_recv,
    edge_send,
    edge_recv,
):
    band = lax.axis_index("band")
    shard = lax.axis_index("tm")
    depth = shards // side
    sx, sz = lax.div(shard, side), lax.rem(shard, side)
    samples = tod.shape[2]
    blocks = samples // PIX
    share = REACH
    span = bands * share
    has_left, has_right = shard > 0, shard < shards - 1
    left, right = lax.rem(shard + shards - 1, shards), lax.rem(shard + 1, shards)

    def shard_peer(i):
        return lax.rem(sx + i // side, depth) * side + lax.rem(sz + i % side, side)

    def hops(i):
        dx, dz = i // side, i % side
        return min(dx, depth - dx) + min(dz, side - dz)

    loads = []
    for n, (source, target) in enumerate(
        (
            (owner_hbm, owner),
            (tile_row_hbm, tile_row),
            (counts_hbm, counts),
            (mixing_hbm, mixing),
            (weights_hbm, weights),
            (taps_hbm, taps),
            (beam_rows_hbm, beam_rows),
            (beam_cols_hbm, beam_cols),
        )
    ):
        loads.append(pltpu.make_async_copy(source, target, small_sem.at[n]))
        loads[-1].start()
    load = pltpu.make_async_copy(tod.at[0], x.at[:, pl.ds(2 * HALF, samples)], load_sem)
    load.start()

    order = sorted(range(1, shards), key=lambda i: -hops(i))

    barrier = pltpu.get_barrier_semaphore()
    for i in order:
        pl.semaphore_signal(barrier, 1, device_id=(band, shard_peer(i)), device_id_type=MESH)
    for i in range(1, bands):
        pl.semaphore_signal(barrier, 1, device_id=(lax.rem(band + i, bands), shard), device_id_type=MESH)

    @pl.when((band == 0) & has_left)
    def _():
        for b in range(1, bands):
            pl.semaphore_signal(barrier, 1, device_id=(b, left), device_id_type=MESH)

    @pl.when((band == bands - 1) & has_right)
    def _():
        for b in range(bands - 1):
            pl.semaphore_signal(barrier, 1, device_id=(b, right), device_id_type=MESH)

    before[...] = jnp.zeros_like(before)
    for start in (0, samples + 2 * HALF):
        x[:, pl.ds(start, 2 * HALF)] = jnp.zeros((x.shape[0], 2 * HALF), BF16)

    row_i, lane_i = iota((blocks, blocks), 0), iota((blocks, blocks), 1)
    diagonal = row_i == lane_i
    for copy in loads[:4]:
        copy.wait()
    owner_row = owner[0:1, :]
    owner_col = jnp.sum(jnp.where(diagonal, owner_row, 0), axis=1, keepdims=True)
    same = (owner_col == owner_row) & (row_i < lane_i)
    rank_row = jnp.sum(jnp.where(same, 1, 0), axis=0, keepdims=True)
    ox, oz = owner_row // side, owner_row % side
    group = ((ox - sx + depth) % depth) * side + (oz - sz + side) % side
    slot_row = group * CAP + rank_row
    kept = iota((1, blocks), 1) < counts[0:1, 0:1]
    slots = shards * CAP
    pick = jnp.where((iota((slots, blocks), 0) == slot_row) & kept, 1.0, 0.0).astype(BF16)
    row_col = jnp.sum(jnp.where(diagonal, tile_row[0:1, :], 0), axis=1, keepdims=True)
    row_hot = jnp.where(iota((blocks, PIX), 1) == row_col, 1.0, 0.0).astype(BF16)
    meta = dot(pick, row_hot)
    meta_out[...] = meta
    meta_in[0:CAP, :] = meta[0:CAP, :]
    mix = jnp.concatenate(
        [jnp.broadcast_to(mixing[0, :, c : c + 1], (NBEAM, PIX)) for c in range(NCOMP)], axis=0
    )
    mix_out[...] = mix
    mix_in[0] = mix

    for copy in loads[4:]:
        copy.wait()
    lag_table(taps, weights, table)
    load.wait()

    even[...] = lagged_sums(x, table, blocks + STEP, (0, 1))
    odd[...] = lagged_sums(x, table, 0, (2, 3))
    add_diagonals(even, here, before, blocks + STEP)

    def two_chunks(i, carry):
        block = pl.multiple_of(STEP + 2 * STEP * i, STEP)
        even[...] = lagged_sums(x, table, block, ALL)
        add_diagonals(odd, here, before, pl.multiple_of(block - STEP, STEP))
        odd[...] = lagged_sums(x, table, pl.multiple_of(block + STEP, STEP), ALL)
        add_diagonals(even, here, before, block)
        return carry

    lax.fori_loop(0, 2, two_chunks, 0)
    overhang[0] = here[0:STEP, :] + before[pl.ds(1, STEP), :]
    overhang[1] = here[pl.ds(blocks + STEP, STEP), :] + before[pl.ds(blocks + STEP + 1, STEP), :]

    pl.semaphore_wait(
        barrier,
        shards
        - 1
        + bands
        - 1
        + jnp.where((band != 0) & has_right, 1, 0)
        + jnp.where((band != bands - 1) & has_left, 1, 0),
    )

    to_left = pltpu.make_async_remote_copy(
        overhang.at[0],
        arrived.at[1],
        halo_send.at[0],
        halo_recv.at[1],
        device_id=(band, left),
        device_id_type=MESH,
    )
    to_right = pltpu.make_async_remote_copy(
        overhang.at[1],
        arrived.at[0],
        halo_send.at[1],
        halo_recv.at[0],
        device_id=(band, right),
        device_id_type=MESH,
    )

    @pl.when(has_right)
    def _():
        to_right.start()

    @pl.when(has_left)
    def _():
        to_left.start()

    def to_shards(source, target, which):
        for i in order:
            pltpu.make_async_remote_copy(
                source.at[pl.ds(CAP * i, CAP)],
                target.at[pl.ds(CAP * i, CAP)],
                peer_send.at[which],
                peer_recv.at[which],
                device_id=(band, shard_peer(i)),
                device_id_type=MESH,
            ).start()

    def from_shards(ref, sem):
        part = ref.at[pl.ds(CAP, slots - CAP)]
        pltpu.make_async_copy(part, part, sem).wait()

    to_shards(meta_out, meta_in, 0)
    for i in range(1, bands):
        pltpu.make_async_remote_copy(
            mix_out,
            mix_in.at[i],
            band_send.at[0, i],
            band_recv.at[0, i],
            device_id=(lax.rem(band + i, bands), shard),
            device_id_type=MESH,
        ).start()

    lax.fori_loop(2, blocks // (2 * STEP), two_chunks, 0)
    add_diagonals(odd, here, before, blocks)

    for side_of, exists in enumerate((has_left, has_right)):

        @pl.when(exists)
        def _(side_of=side_of):
            part = arrived.at[side_of]
            pltpu.make_async_copy(part, part, halo_recv.at[side_of]).wait()

        @pl.when(jnp.logical_not(exists))
        def _(side_of=side_of):
            arrived[side_of] = jnp.zeros((STEP, PIX), F32)

    own = here[pl.ds(STEP, blocks), :] + before[pl.ds(STEP + 1, blocks), :]
    block_values = jnp.concatenate(
        [own[0:STEP] + arrived[0], own[STEP : blocks - STEP], own[blocks - STEP :] + arrived[1]],
        axis=0,
    )
    value_high, value_low = split(block_values)
    values = dot(pick, value_high) + dot(pick, value_low)
    vals_out[...] = values
    vals_in[0:CAP, :] = values[0:CAP, :]
    to_shards(vals_out, vals_in, 1)

    long = span + 2 * REACH
    row_mats = jnp.concatenate(
        [band_rows(beam_rows[0, k : k + 1, :], long, BEAM - 1) for k in range(NBEAM)],
        axis=0,
    )
    rows_high, rows_low = split(row_mats)
    from_shards(meta_in, peer_recv.at[0])
    hot = meta_in[...].astype(BF16)
    slot_high = dot_nt(rows_high, hot).astype(BF16)
    slot_low = dot_nt(rows_low, hot).astype(BF16)
    cols = [split(band_rows(beam_cols[0, k : k + 1, :], PIX, REACH)) for k in range(NBEAM)]

    from_shards(vals_in, peer_recv.at[1])
    in_high, in_low = split(vals_in[...])
    rowed = dot(slot_high, in_high) + dot(slot_high, in_low) + dot(slot_low, in_high)
    for k in range(NBEAM):
        rowed_high, rowed_low = split(rowed[long * k : long * (k + 1), :])
        col_high, col_low = cols[k]
        wide[k] = (
            dot_nt(rowed_high, col_high) + dot_nt(rowed_low, col_high) + dot_nt(rowed_high, col_low)
        )

    below = pltpu.make_async_remote_copy(
        wide.at[:, pl.ds(REACH + span, REACH), :],
        edge.at[lax.rem(bands - band, bands)],
        edge_send.at[0],
        edge_recv.at[lax.rem(bands - band, bands)],
        device_id=(0, right),
        device_id_type=MESH,
    )
    above = pltpu.make_async_remote_copy(
        wide.at[:, pl.ds(0, REACH), :],
        edge.at[bands - 1 - band],
        edge_send.at[1],
        edge_recv.at[bands - 1 - band],
        device_id=(bands - 1, left),
        device_id_type=MESH,
    )

    @pl.when(has_right)
    def _():
        below.start()

    @pl.when(has_left)
    def _():
        above.start()

    sends = []
    for i in range(1, bands):
        peer = lax.rem(band + i, bands)
        copy = pltpu.make_async_remote_copy(
            wide.at[:, pl.ds(pl.multiple_of(REACH + share * peer, REACH), share), :],
            mine.at[i],
            band_send.at[1, i],
            band_recv.at[1, i],
            device_id=(peer, shard),
            device_id_type=MESH,
        )
        copy.start()
        sends.append(copy)
    mine[0] = wide[:, pl.ds(pl.multiple_of(REACH + share * band, REACH), share), :]
    for i in range(1, bands):
        pltpu.make_async_copy(mix_in.at[i], mix_in.at[i], band_recv.at[0, i]).wait()
    for i in range(1, bands):
        pltpu.make_async_copy(mine.at[i], mine.at[i], band_recv.at[1, i]).wait()

    @pl.when(((band == 0) & has_left) | ((band == bands - 1) & has_right))
    def _():
        for i in range(bands):
            pltpu.make_async_copy(edge.at[i], edge.at[i], edge_recv.at[i]).wait()
        mine[...] += edge[...]

    for c in range(NCOMP):
        total = None
        for i in range(bands):
            for k in range(NBEAM):
                term = mix_in[i, c * NBEAM + k : c * NBEAM + k + 1, :] * mine[i, k]
                total = term if total is None else total + term
        out[c, 0] = total

    @pl.when(has_right)
    def _():
        to_right.wait_send()
        below.wait_send()

    @pl.when(has_left)
    def _():
        to_left.wait_send()
        above.wait_send()

    from_shards(meta_out, peer_send.at[0])
    from_shards(vals_out, peer_send.at[1])
    for i in range(1, bands):
        pltpu.make_async_copy(mix_out, mix_out, band_send.at[0, i]).wait()
    for copy in sends:
        copy.wait_send()


def on_device(
    tod, filter_taps, det_weights, owner, tile_row, block_counts, beam_rows, beam_cols, mixing
):
    bands, shards = lax.axis_size("band"), lax.axis_size("tm")
    side = 8 if shards >= 16 else shards // 2
    det, samples = tod.shape[1:]
    slots = shards * CAP
    long = bands * REACH + 2 * REACH
    blocks = samples // PIX
    vmem = pl.BlockSpec(memory_space=pltpu.VMEM)
    return pl.pallas_call(
        functools.partial(kernel, bands, shards, side),
        out_shape=jax.ShapeDtypeStruct((NCOMP, 1, REACH, PIX), F32),
        in_specs=[pl.BlockSpec(memory_space=pltpu.HBM)] * 9,
        out_specs=vmem,
        scratch_shapes=[
            pltpu.VMEM(filter_taps.shape, BF16),
            pltpu.VMEM((1, det), F32),
            pltpu.VMEM((1, blocks), jnp.int32),
            pltpu.VMEM((1, blocks), jnp.int32),
            pltpu.VMEM((1, 1), jnp.int32),
            pltpu.VMEM(beam_rows.shape, F32),
            pltpu.VMEM(beam_cols.shape, F32),
            pltpu.VMEM((1, NBEAM, NCOMP), F32),
            pltpu.VMEM((det, samples + 4 * HALF), BF16),
            pltpu.VMEM((2 * PIX + 16, LAGS * det), BF16),
            pltpu.VMEM((blocks + 3 * STEP, PIX), F32),
            pltpu.VMEM((blocks + 3 * STEP, PIX), F32),
            pltpu.VMEM((2 * PIX + 16, CHUNK), F32),
            pltpu.VMEM((2 * PIX + 16, CHUNK), F32),
            pltpu.VMEM((2, STEP, PIX), F32),
            pltpu.VMEM((2, STEP, PIX), F32),
            pltpu.VMEM((slots, PIX), F32),
            pltpu.VMEM((slots, PIX), F32),
            pltpu.VMEM((slots, PIX), F32),
            pltpu.VMEM((slots, PIX), F32),
            pltpu.VMEM((NCOMP * NBEAM, PIX), F32),
            pltpu.VMEM((bands, NCOMP * NBEAM, PIX), F32),
            pltpu.VMEM((NBEAM, long, PIX), F32),
            pltpu.VMEM((bands, NBEAM, REACH, PIX), F32),
            pltpu.VMEM((bands, NBEAM, REACH, PIX), F32),
            pltpu.SemaphoreType.DMA,
            pltpu.SemaphoreType.DMA((8,)),
            pltpu.SemaphoreType.DMA((2,)),
            pltpu.SemaphoreType.DMA((2,)),
            pltpu.SemaphoreType.DMA((2,)),
            pltpu.SemaphoreType.DMA((2,)),
            pltpu.SemaphoreType.DMA((2, bands)),
            pltpu.SemaphoreType.DMA((2, bands)),
            pltpu.SemaphoreType.DMA((2,)),
            pltpu.SemaphoreType.DMA((bands,)),
        ],
        compiler_params=pltpu.CompilerParams(
            collective_id=0, has_side_effects=True, vmem_limit_bytes=67043328
        ),
    )(
        tod,
        filter_taps,
        det_weights,
        owner.reshape(1, blocks),
        tile_row,
        block_counts,
        beam_rows,
        beam_cols,
        mixing.transpose(1, 2, 0),
    )


def solution(mesh):
    placed = (
        P("band", None, "tm"),
        P("band", None, None),
        P("band", None),
        P("band", "tm", None),
        P("band", "tm"),
        P("band", "tm"),
        P("band", None, None),
        P("band", None, None),
        P(None, "band", None),
    )
    return jax.shard_map(
        on_device,
        mesh=mesh,
        in_specs=placed,
        out_specs=P(None, "tm", "band", None),
        check_vma=False,
    )
```

```python
import functools

import jax
import jax.numpy as jnp
from jax import lax
from jax.experimental import pallas as pl
from jax.experimental.pallas import tpu as pltpu
from jax.sharding import PartitionSpec as P

PIX = 128
CAP = 8
HALF = 1024
LAGS = 16
BEAM = 33
REACH = 16
NBEAM = 2
NCOMP = 4
CHUNK = 1024
PARTS = 4
STEP = CHUNK // PIX
MESH = pl.DeviceIdType.MESH
F32 = jnp.float32
BF16 = jnp.bfloat16
NT = (((1,), (1,)), ((), ()))


def iota(shape, axis):
    return lax.broadcasted_iota(jnp.int32, shape, axis)


def split(value):
    high = value.astype(BF16)
    return high, (value - high.astype(F32)).astype(BF16)


def dot(a, b):
    return jnp.dot(a, b, preferred_element_type=F32)


def dot_nt(a, b):
    return lax.dot_general(a, b, NT, preferred_element_type=F32)


def lag_table(taps, weights, table):
    det = taps.shape[1]
    eye = iota((det, det), 0) == iota((det, det), 1)
    column = jnp.sum(jnp.where(eye, weights[0:1, :], 0.0), axis=1, keepdims=True)
    flip = jnp.where(iota((PIX, PIX), 0) + iota((PIX, PIX), 1) == PIX - 1, 1.0, 0.0).astype(BF16)
    pair = 2 * PIX
    for j in range(LAGS // 2):
        both = jnp.concatenate(
            [taps[0, :, pl.ds(pair * j + PIX * e, PIX)].astype(F32) * column for e in range(2)],
            axis=0,
        )
        turned = dot_nt(flip, jnp.concatenate(split(both), axis=0)).astype(BF16)
        lanes = pl.ds(2 * det * j, 2 * det)
        table[0:PIX, lanes] = turned[:, 0 : 2 * det]
        table[PIX : 2 * PIX, lanes] = turned[:, 2 * det :]
    last = taps[0, :, 2 * HALF : 2 * HALF + 1].astype(F32) * column
    last_high = last.astype(BF16).astype(F32)
    spot = iota((det, 2 * det), 1) == iota((det, 2 * det), 0) + det
    row_high = jnp.sum(jnp.where(spot, last_high, 0.0), axis=0, keepdims=True)
    row_low = jnp.sum(jnp.where(spot, last - last_high, 0.0), axis=0, keepdims=True)
    rows = iota((16, 2 * det), 0)
    rest = (LAGS - 2) * det
    table[2 * PIX : 2 * PIX + 16, 0:rest] = jnp.zeros((16, rest), BF16)
    table[2 * PIX : 2 * PIX + 16, rest : rest + 2 * det] = jnp.where(
        rows == 0, row_high, jnp.where(rows == 1, row_low, 0.0)
    ).astype(BF16)


def lagged_sums(x, table, sums, block, blocks):
    det = x.shape[0]
    top = 2 * PIX
    for piece in range(2):
        first = block + piece * STEP // 2
        lanes = pl.ds(piece * CHUNK // 2, CHUNK // 2)
        total = last = None
        for q in (3, 2, 1, 0):
            if first + STEP // 2 + 4 * q + 3 <= LAGS or first + 4 * q >= blocks + LAGS:
                continue
            window = jnp.concatenate(
                [x[:, pl.ds(PIX * (first + 4 * q + e), CHUNK // 2)] for e in range(4)], axis=0
            )
            rows = top + 16 if q == 3 else top
            part = dot(table[0:rows, 4 * det * q : 4 * det * (q + 1)], window)
            if q == 3:
                last = part[top:]
            total = part[0:top] if total is None else total + part[0:top]
        shape = (top, CHUNK // 2)
        sums[0:top, lanes] = jnp.zeros(shape, F32) if total is None else total
        sums[pl.ds(top, 16), lanes] = jnp.zeros((16, CHUNK // 2), F32) if last is None else last


def add_diagonals(sums, here, before, block):
    keeps = iota((PIX, PIX), 1) <= iota((PIX, PIX), 0)
    prior = None
    for k in range(STEP):
        lanes = pl.ds(PIX * k, PIX)
        turned = pltpu.roll(
            sums[0:PIX, lanes] + sums[PIX : 2 * PIX, lanes], 1, 1, stride=1, stride_axis=0
        )
        final = sums[2 * PIX : 2 * PIX + 1, lanes] + sums[2 * PIX + 1 : 2 * PIX + 2, lanes]
        merged = jnp.where(keeps, 0.0 if k == 0 else prior, turned)
        done = jnp.sum(merged, axis=0, keepdims=True) + final
        if k == 0:
            before[pl.ds(block, 1), :] = done
        else:
            here[pl.ds(block + k - 1, 1), :] = done
        prior = turned
    here[pl.ds(block + STEP - 1, 1), :] = jnp.sum(
        jnp.where(keeps, prior, 0.0), axis=0, keepdims=True
    )


def band_rows(profile, out_rows, shift):
    wide = jnp.concatenate([profile, jnp.zeros((1, PIX - BEAM), F32)], axis=1)
    spread = jnp.broadcast_to(wide, (out_rows, PIX))
    turned = pltpu.roll(spread, PIX - shift, 1, stride=1, stride_axis=0)
    tap = iota((out_rows, PIX), 1) - iota((out_rows, PIX), 0) + shift
    return jnp.where((tap >= 0) & (tap < BEAM), turned, 0.0)


def kernel(
    bands,
    shards,
    side,
    tod,
    taps_hbm,
    weights_hbm,
    owner_hbm,
    tile_row_hbm,
    beam_rows_hbm,
    beam_cols_hbm,
    mixing_hbm,
    counts,
    out,
    taps,
    weights,
    owner,
    tile_row,
    beam_rows,
    beam_cols,
    mixing,
    x,
    table,
    here,
    before,
    even,
    odd,
    overhang,
    arrived,
    meta_out,
    meta_in,
    vals_out,
    vals_in,
    mix_out,
    mix_in,
    wide,
    mine,
    edge,
    load_sem,
    small_sem,
    halo_send,
    halo_recv,
    peer_send,
    peer_recv,
    band_send,
    band_recv,
    edge_send,
    edge_recv,
):
    band = lax.axis_index("band")
    shard = lax.axis_index("tm")
    depth = shards // side
    sx, sz = lax.div(shard, side), lax.rem(shard, side)
    samples = tod.shape[2]
    blocks = samples // PIX
    share = REACH
    span = bands * share
    has_left, has_right = shard > 0, shard < shards - 1
    left, right = lax.rem(shard + shards - 1, shards), lax.rem(shard + 1, shards)

    def shard_peer(i):
        return lax.rem(sx + i // side, depth) * side + lax.rem(sz + i % side, side)

    def hops(i):
        dx, dz = i // side, i % side
        return min(dx, depth - dx) + min(dz, side - dz)

    loads = []
    for n, (source, target) in enumerate(
        (
            (owner_hbm, owner),
            (tile_row_hbm, tile_row),
            (mixing_hbm, mixing),
            (weights_hbm, weights),
            (taps_hbm, taps),
            (beam_rows_hbm, beam_rows),
            (beam_cols_hbm, beam_cols),
        )
    ):
        loads.append(pltpu.make_async_copy(source, target, small_sem.at[n]))
        loads[-1].start()
    loads_x = []
    for n in range(PARTS):
        rows = pl.ds(n * tod.shape[1] // PARTS, tod.shape[1] // PARTS)
        loads_x.append(
            pltpu.make_async_copy(
                tod.at[0, rows], x.at[rows, pl.ds(2 * HALF, samples)], load_sem.at[n]
            )
        )
        loads_x[-1].start()

    order = sorted(range(1, shards), key=lambda i: -hops(i))

    barrier = pltpu.get_barrier_semaphore()
    for i in order:
        pl.semaphore_signal(barrier, 1, device_id=(band, shard_peer(i)), device_id_type=MESH)
    for i in range(1, bands):
        pl.semaphore_signal(barrier, 1, device_id=(lax.rem(band + i, bands), shard), device_id_type=MESH)

    @pl.when((band == 0) & has_left)
    def _():
        for b in range(1, bands):
            pl.semaphore_signal(barrier, 1, device_id=(b, left), device_id_type=MESH)

    @pl.when((band == bands - 1) & has_right)
    def _():
        for b in range(bands - 1):
            pl.semaphore_signal(barrier, 1, device_id=(b, right), device_id_type=MESH)

    before[...] = jnp.zeros_like(before)
    for start in (0, samples + 2 * HALF):
        x[:, pl.ds(start, 2 * HALF)] = jnp.zeros((x.shape[0], 2 * HALF), BF16)

    for copy in loads:
        copy.wait()

    row_i, lane_i = iota((blocks, blocks), 0), iota((blocks, blocks), 1)
    diagonal = row_i == lane_i
    owner_row = owner[0:1, :]
    owner_col = jnp.sum(jnp.where(diagonal, owner_row, 0), axis=1, keepdims=True)
    same = (owner_col == owner_row) & (row_i < lane_i)
    rank_row = jnp.sum(jnp.where(same, 1, 0), axis=0, keepdims=True)
    ox, oz = owner_row // side, owner_row % side
    group = ((ox - sx + depth) % depth) * side + (oz - sz + side) % side
    slot_row = group * CAP + rank_row
    kept = iota((1, blocks), 1) < counts[0, 0]
    slots = shards * CAP
    pick = jnp.where((iota((slots, blocks), 0) == slot_row) & kept, 1.0, 0.0).astype(BF16)
    row_col = jnp.sum(jnp.where(diagonal, tile_row[0:1, :], 0), axis=1, keepdims=True)
    row_hot = jnp.where(iota((blocks, PIX), 1) == row_col, 1.0, 0.0).astype(BF16)
    meta = dot(pick, row_hot)
    meta_out[...] = meta
    meta_in[0:CAP, :] = meta[0:CAP, :]
    mix = jnp.concatenate(
        [jnp.broadcast_to(mixing[0, :, c : c + 1], (NBEAM, PIX)) for c in range(NCOMP)], axis=0
    )
    mix_out[...] = mix
    mix_in[0] = mix

    lag_table(taps, weights, table)
    for copy in loads_x:
        copy.wait()

    def sums_of(target, block):
        lagged_sums(x, table, target, block, blocks)

    sums_of(even, blocks + STEP)
    sums_of(odd, 0)
    add_diagonals(even, here, before, blocks + STEP)

    def two_chunks(block):
        sums_of(even, block)
        add_diagonals(odd, here, before, block - STEP)
        sums_of(odd, block + STEP)
        add_diagonals(even, here, before, block)

    for i in range(2):
        two_chunks(STEP + 2 * STEP * i)
    overhang[0] = here[0:STEP, :] + before[pl.ds(1, STEP), :]
    overhang[1] = here[pl.ds(blocks + STEP, STEP), :] + before[pl.ds(blocks + STEP + 1, STEP), :]

    pl.semaphore_wait(
        barrier,
        shards
        - 1
        + bands
        - 1
        + jnp.where((band != 0) & has_right, 1, 0)
        + jnp.where((band != bands - 1) & has_left, 1, 0),
    )

    to_left = pltpu.make_async_remote_copy(
        overhang.at[0],
        arrived.at[1],
        halo_send.at[0],
        halo_recv.at[1],
        device_id=(band, left),
        device_id_type=MESH,
    )
    to_right = pltpu.make_async_remote_copy(
        overhang.at[1],
        arrived.at[0],
        halo_send.at[1],
        halo_recv.at[0],
        device_id=(band, right),
        device_id_type=MESH,
    )

    @pl.when(has_right)
    def _():
        to_right.start()

    @pl.when(has_left)
    def _():
        to_left.start()

    def to_shards(source, target, which):
        for i in order:
            pltpu.make_async_remote_copy(
                source.at[pl.ds(CAP * i, CAP)],
                target.at[pl.ds(CAP * i, CAP)],
                peer_send.at[which],
                peer_recv.at[which],
                device_id=(band, shard_peer(i)),
                device_id_type=MESH,
            ).start()

    def from_shards(ref, sem):
        part = ref.at[pl.ds(CAP, slots - CAP)]
        pltpu.make_async_copy(part, part, sem).wait()

    to_shards(meta_out, meta_in, 0)
    for i in range(1, bands):
        pltpu.make_async_remote_copy(
            mix_out,
            mix_in.at[i],
            band_send.at[0, i],
            band_recv.at[0, i],
            device_id=(lax.rem(band + i, bands), shard),
            device_id_type=MESH,
        ).start()

    for i in range(2, blocks // (2 * STEP)):
        two_chunks(STEP + 2 * STEP * i)
    add_diagonals(odd, here, before, blocks)

    for side_of, exists in enumerate((has_left, has_right)):

        @pl.when(exists)
        def _(side_of=side_of):
            part = arrived.at[side_of]
            pltpu.make_async_copy(part, part, halo_recv.at[side_of]).wait()

        @pl.when(jnp.logical_not(exists))
        def _(side_of=side_of):
            arrived[side_of] = jnp.zeros((STEP, PIX), F32)

    own = here[pl.ds(STEP, blocks), :] + before[pl.ds(STEP + 1, blocks), :]
    block_values = jnp.concatenate(
        [own[0:STEP] + arrived[0], own[STEP : blocks - STEP], own[blocks - STEP :] + arrived[1]],
        axis=0,
    )
    value_high, value_low = split(block_values)
    values = dot(pick, value_high) + dot(pick, value_low)
    vals_out[...] = values
    vals_in[0:CAP, :] = values[0:CAP, :]
    to_shards(vals_out, vals_in, 1)

    long = span + 2 * REACH
    row_mats = jnp.concatenate(
        [band_rows(beam_rows[0, k : k + 1, :], long, BEAM - 1) for k in range(NBEAM)],
        axis=0,
    )
    rows_high, rows_low = split(row_mats)
    from_shards(meta_in, peer_recv.at[0])
    hot = meta_in[...].astype(BF16)
    slot_high = dot_nt(rows_high, hot).astype(BF16)
    slot_low = dot_nt(rows_low, hot).astype(BF16)
    cols = [split(band_rows(beam_cols[0, k : k + 1, :], PIX, REACH)) for k in range(NBEAM)]

    from_shards(vals_in, peer_recv.at[1])
    in_high, in_low = split(vals_in[...])
    rowed = dot(slot_high, in_high) + dot(slot_high, in_low) + dot(slot_low, in_high)
    for k in range(NBEAM):
        rowed_high, rowed_low = split(rowed[long * k : long * (k + 1), :])
        col_high, col_low = cols[k]
        wide[k] = (
            dot_nt(rowed_high, col_high) + dot_nt(rowed_low, col_high) + dot_nt(rowed_high, col_low)
        )

    below = pltpu.make_async_remote_copy(
        wide.at[:, pl.ds(REACH + span, REACH), :],
        edge.at[lax.rem(bands - band, bands)],
        edge_send.at[0],
        edge_recv.at[lax.rem(bands - band, bands)],
        device_id=(0, right),
        device_id_type=MESH,
    )
    above = pltpu.make_async_remote_copy(
        wide.at[:, pl.ds(0, REACH), :],
        edge.at[bands - 1 - band],
        edge_send.at[1],
        edge_recv.at[bands - 1 - band],
        device_id=(bands - 1, left),
        device_id_type=MESH,
    )

    @pl.when(has_right)
    def _():
        below.start()

    @pl.when(has_left)
    def _():
        above.start()

    sends = []
    for i in range(1, bands):
        peer = lax.rem(band + i, bands)
        copy = pltpu.make_async_remote_copy(
            wide.at[:, pl.ds(pl.multiple_of(REACH + share * peer, REACH), share), :],
            mine.at[i],
            band_send.at[1, i],
            band_recv.at[1, i],
            device_id=(peer, shard),
            device_id_type=MESH,
        )
        copy.start()
        sends.append(copy)
    mine[0] = wide[:, pl.ds(pl.multiple_of(REACH + share * band, REACH), share), :]
    for i in range(1, bands):
        pltpu.make_async_copy(mix_in.at[i], mix_in.at[i], band_recv.at[0, i]).wait()
    for i in range(1, bands):
        pltpu.make_async_copy(mine.at[i], mine.at[i], band_recv.at[1, i]).wait()

    @pl.when(((band == 0) & has_left) | ((band == bands - 1) & has_right))
    def _():
        for i in range(bands):
            pltpu.make_async_copy(edge.at[i], edge.at[i], edge_recv.at[i]).wait()
        mine[...] += edge[...]

    for c in range(NCOMP):
        total = None
        for i in range(bands):
            for k in range(NBEAM):
                term = mix_in[i, c * NBEAM + k : c * NBEAM + k + 1, :] * mine[i, k]
                total = term if total is None else total + term
        out[c, 0] = total

    @pl.when(has_right)
    def _():
        to_right.wait_send()
        below.wait_send()

    @pl.when(has_left)
    def _():
        to_left.wait_send()
        above.wait_send()

    from_shards(meta_out, peer_send.at[0])
    from_shards(vals_out, peer_send.at[1])
    for i in range(1, bands):
        pltpu.make_async_copy(mix_out, mix_out, band_send.at[0, i]).wait()
    for copy in sends:
        copy.wait_send()


def on_device(
    tod, filter_taps, det_weights, owner, tile_row, block_counts, beam_rows, beam_cols, mixing
):
    bands, shards = lax.axis_size("band"), lax.axis_size("tm")
    side = 8 if shards >= 16 else shards // 2
    det, samples = tod.shape[1:]
    slots = shards * CAP
    long = bands * REACH + 2 * REACH
    blocks = samples // PIX
    vmem = pl.BlockSpec(memory_space=pltpu.VMEM)
    return pl.pallas_call(
        functools.partial(kernel, bands, shards, side),
        out_shape=jax.ShapeDtypeStruct((NCOMP, 1, REACH, PIX), F32),
        in_specs=[pl.BlockSpec(memory_space=pltpu.HBM)] * 8
        + [pl.BlockSpec(memory_space=pltpu.SMEM)],
        out_specs=vmem,
        scratch_shapes=[
            pltpu.VMEM(filter_taps.shape, BF16),
            pltpu.VMEM((1, det), F32),
            pltpu.VMEM((1, blocks), jnp.int32),
            pltpu.VMEM((1, blocks), jnp.int32),
            pltpu.VMEM(beam_rows.shape, F32),
            pltpu.VMEM(beam_cols.shape, F32),
            pltpu.VMEM((1, NBEAM, NCOMP), F32),
            pltpu.VMEM((det, samples + 4 * HALF), BF16),
            pltpu.VMEM((2 * PIX + 16, LAGS * det), BF16),
            pltpu.VMEM((blocks + 3 * STEP, PIX), F32),
            pltpu.VMEM((blocks + 3 * STEP, PIX), F32),
            pltpu.VMEM((2 * PIX + 16, CHUNK), F32),
            pltpu.VMEM((2 * PIX + 16, CHUNK), F32),
            pltpu.VMEM((2, STEP, PIX), F32),
            pltpu.VMEM((2, STEP, PIX), F32),
            pltpu.VMEM((slots, PIX), F32),
            pltpu.VMEM((slots, PIX), F32),
            pltpu.VMEM((slots, PIX), F32),
            pltpu.VMEM((slots, PIX), F32),
            pltpu.VMEM((NCOMP * NBEAM, PIX), F32),
            pltpu.VMEM((bands, NCOMP * NBEAM, PIX), F32),
            pltpu.VMEM((NBEAM, long, PIX), F32),
            pltpu.VMEM((bands, NBEAM, REACH, PIX), F32),
            pltpu.VMEM((bands, NBEAM, REACH, PIX), F32),
            pltpu.SemaphoreType.DMA((PARTS,)),
            pltpu.SemaphoreType.DMA((7,)),
            pltpu.SemaphoreType.DMA((2,)),
            pltpu.SemaphoreType.DMA((2,)),
            pltpu.SemaphoreType.DMA((2,)),
            pltpu.SemaphoreType.DMA((2,)),
            pltpu.SemaphoreType.DMA((2, bands)),
            pltpu.SemaphoreType.DMA((2, bands)),
            pltpu.SemaphoreType.DMA((2,)),
            pltpu.SemaphoreType.DMA((bands,)),
        ],
        compiler_params=pltpu.CompilerParams(
            collective_id=0, has_side_effects=True, vmem_limit_bytes=50331648
        ),
    )(
        *(pltpu.with_memory_space_constraint(v, pltpu.HBM) for v in (tod,
        filter_taps,
        det_weights,
        owner.reshape(1, blocks),
        tile_row,
        beam_rows,
        beam_cols,
        mixing.transpose(1, 2, 0),)),
        block_counts,
    )


def solution(mesh):
    placed = (
        P("band", None, "tm"),
        P("band", None, None),
        P("band", None),
        P("band", "tm", None),
        P("band", "tm"),
        P("band", "tm"),
        P("band", None, None),
        P("band", None, None),
        P(None, "band", None),
    )
    return jax.shard_map(
        on_device,
        mesh=mesh,
        in_specs=placed,
        out_specs=P(None, "tm", "band", None),
        check_vma=False,
    )
```

```python
import functools

import jax
import jax.numpy as jnp
from jax import lax
from jax.experimental import pallas as pl
from jax.experimental.pallas import tpu as pltpu
from jax.sharding import PartitionSpec as P

PIX = 128
CAP = 8
HALF = 1024
LAGS = 16
BEAM = 33
REACH = 16
NBEAM = 2
NCOMP = 4
CHUNK = 1024
PARTS = 4
STEP = CHUNK // PIX
MESH = pl.DeviceIdType.MESH
F32 = jnp.float32
BF16 = jnp.bfloat16
NT = (((1,), (1,)), ((), ()))


def iota(shape, axis):
    return lax.broadcasted_iota(jnp.int32, shape, axis)


def split(value):
    high = value.astype(BF16)
    return high, (value - high.astype(F32)).astype(BF16)


def dot(a, b):
    return jnp.dot(a, b, preferred_element_type=F32)


def dot_nt(a, b):
    return lax.dot_general(a, b, NT, preferred_element_type=F32)


def lag_table(taps, weights, table):
    det = taps.shape[1]
    eye = iota((det, det), 0) == iota((det, det), 1)
    column = jnp.sum(jnp.where(eye, weights[0:1, :], 0.0), axis=1, keepdims=True)
    flip = jnp.where(iota((PIX, PIX), 0) + iota((PIX, PIX), 1) == PIX - 1, 1.0, 0.0).astype(BF16)
    pair = 2 * PIX
    for j in range(LAGS // 2):
        both = jnp.concatenate(
            [taps[0, :, pl.ds(pair * j + PIX * e, PIX)].astype(F32) * column for e in range(2)],
            axis=0,
        )
        turned = dot_nt(flip, jnp.concatenate(split(both), axis=0)).astype(BF16)
        lanes = pl.ds(2 * det * j, 2 * det)
        table[0:PIX, lanes] = turned[:, 0 : 2 * det]
        table[PIX : 2 * PIX, lanes] = turned[:, 2 * det :]
    last = taps[0, :, 2 * HALF : 2 * HALF + 1].astype(F32) * column
    last_high = last.astype(BF16).astype(F32)
    spot = iota((det, 2 * det), 1) == iota((det, 2 * det), 0) + det
    row_high = jnp.sum(jnp.where(spot, last_high, 0.0), axis=0, keepdims=True)
    row_low = jnp.sum(jnp.where(spot, last - last_high, 0.0), axis=0, keepdims=True)
    rows = iota((16, 2 * det), 0)
    rest = (LAGS - 2) * det
    table[2 * PIX : 2 * PIX + 16, 0:rest] = jnp.zeros((16, rest), BF16)
    table[2 * PIX : 2 * PIX + 16, rest : rest + 2 * det] = jnp.where(
        rows == 0, row_high, jnp.where(rows == 1, row_low, 0.0)
    ).astype(BF16)


def lagged_sums(x, table, sums, block, blocks):
    det = x.shape[0]
    top = 2 * PIX
    for piece in range(2):
        first = block + piece * STEP // 2
        lanes = pl.ds(piece * CHUNK // 2, CHUNK // 2)
        total = last = None
        for q in (3, 2, 1, 0):
            if first + STEP // 2 + 4 * q + 3 <= LAGS or first + 4 * q >= blocks + LAGS:
                continue
            window = jnp.concatenate(
                [x[:, pl.ds(PIX * (first + 4 * q + e), CHUNK // 2)] for e in range(4)], axis=0
            )
            rows = top + 16 if q == 3 else top
            part = dot(table[0:rows, 4 * det * q : 4 * det * (q + 1)], window)
            if q == 3:
                last = part[top:]
            total = part[0:top] if total is None else total + part[0:top]
        shape = (top, CHUNK // 2)
        sums[0:top, lanes] = jnp.zeros(shape, F32) if total is None else total
        sums[pl.ds(top, 16), lanes] = jnp.zeros((16, CHUNK // 2), F32) if last is None else last


def add_diagonals(sums, here, before, block):
    keeps = iota((PIX, PIX), 1) <= iota((PIX, PIX), 0)
    prior = None
    for k in range(STEP):
        lanes = pl.ds(PIX * k, PIX)
        turned = pltpu.roll(
            sums[0:PIX, lanes] + sums[PIX : 2 * PIX, lanes], 1, 1, stride=1, stride_axis=0
        )
        final = sums[2 * PIX : 2 * PIX + 1, lanes] + sums[2 * PIX + 1 : 2 * PIX + 2, lanes]
        merged = jnp.where(keeps, 0.0 if k == 0 else prior, turned)
        done = jnp.sum(merged, axis=0, keepdims=True) + final
        if k == 0:
            before[pl.ds(block, 1), :] = done
        else:
            here[pl.ds(block + k - 1, 1), :] = done
        prior = turned
    here[pl.ds(block + STEP - 1, 1), :] = jnp.sum(
        jnp.where(keeps, prior, 0.0), axis=0, keepdims=True
    )


def band_rows(profile, out_rows, shift):
    wide = jnp.concatenate([profile, jnp.zeros((1, PIX - BEAM), F32)], axis=1)
    spread = jnp.broadcast_to(wide, (out_rows, PIX))
    turned = pltpu.roll(spread, PIX - shift, 1, stride=1, stride_axis=0)
    tap = iota((out_rows, PIX), 1) - iota((out_rows, PIX), 0) + shift
    return jnp.where((tap >= 0) & (tap < BEAM), turned, 0.0)


def kernel(
    bands,
    shards,
    side,
    tod,
    taps_hbm,
    weights_hbm,
    owner_hbm,
    tile_row_hbm,
    beam_rows_hbm,
    beam_cols_hbm,
    mixing_hbm,
    counts,
    out,
    taps,
    weights,
    owner,
    tile_row,
    beam_rows,
    beam_cols,
    mixing,
    x,
    table,
    here,
    before,
    even,
    odd,
    overhang,
    arrived,
    meta_out,
    meta_in,
    vals_out,
    vals_in,
    mix_out,
    mix_in,
    wide,
    mine,
    edge,
    load_sem,
    small_sem,
    halo_send,
    halo_recv,
    peer_send,
    peer_recv,
    band_send,
    band_recv,
    edge_send,
    edge_recv,
):
    band = lax.axis_index("band")
    shard = lax.axis_index("tm")
    depth = shards // side
    sx, sz = lax.div(shard, side), lax.rem(shard, side)
    samples = tod.shape[2]
    blocks = samples // PIX
    share = REACH
    span = bands * share
    has_left, has_right = shard > 0, shard < shards - 1
    left, right = lax.rem(shard + shards - 1, shards), lax.rem(shard + 1, shards)

    def shard_peer(i):
        return lax.rem(sx + i // side, depth) * side + lax.rem(sz + i % side, side)

    def hops(i):
        dx, dz = i // side, i % side
        return min(dx, depth - dx) + min(dz, side - dz)

    loads = []
    for n, (source, target) in enumerate(
        (
            (owner_hbm, owner),
            (tile_row_hbm, tile_row),
            (mixing_hbm, mixing),
            (weights_hbm, weights),
            (taps_hbm, taps),
            (beam_rows_hbm, beam_rows),
            (beam_cols_hbm, beam_cols),
        )
    ):
        loads.append(pltpu.make_async_copy(source, target, small_sem.at[n]))
        loads[-1].start()
    loads_x = []
    for n in range(PARTS):
        rows = pl.ds(n * tod.shape[1] // PARTS, tod.shape[1] // PARTS)
        loads_x.append(
            pltpu.make_async_copy(
                tod.at[0, rows], x.at[rows, pl.ds(2 * HALF, samples)], load_sem.at[n]
            )
        )
        loads_x[-1].start()

    order = sorted(range(1, shards), key=lambda i: -hops(i))

    barrier = pltpu.get_barrier_semaphore()
    for i in order:
        pl.semaphore_signal(barrier, 1, device_id=(band, shard_peer(i)), device_id_type=MESH)
    for i in range(1, bands):
        pl.semaphore_signal(barrier, 1, device_id=(lax.rem(band + i, bands), shard), device_id_type=MESH)

    @pl.when((band == 0) & has_left)
    def _():
        for b in range(1, bands):
            pl.semaphore_signal(barrier, 1, device_id=(b, left), device_id_type=MESH)

    @pl.when((band == bands - 1) & has_right)
    def _():
        for b in range(bands - 1):
            pl.semaphore_signal(barrier, 1, device_id=(b, right), device_id_type=MESH)

    before[...] = jnp.zeros_like(before)
    for start in (0, samples + 2 * HALF):
        x[:, pl.ds(start, 2 * HALF)] = jnp.zeros((x.shape[0], 2 * HALF), BF16)

    for copy in loads[:3]:
        copy.wait()

    row_i, lane_i = iota((blocks, blocks), 0), iota((blocks, blocks), 1)
    diagonal = row_i == lane_i
    owner_row = owner[0:1, :]
    owner_col = jnp.sum(jnp.where(diagonal, owner_row, 0), axis=1, keepdims=True)
    same = (owner_col == owner_row) & (row_i < lane_i)
    rank_row = jnp.sum(jnp.where(same, 1, 0), axis=0, keepdims=True)
    ox, oz = owner_row // side, owner_row % side
    group = ((ox - sx + depth) % depth) * side + (oz - sz + side) % side
    slot_row = group * CAP + rank_row
    kept = iota((1, blocks), 1) < counts[0, 0]
    slots = shards * CAP
    pick = jnp.where((iota((slots, blocks), 0) == slot_row) & kept, 1.0, 0.0).astype(BF16)
    row_col = jnp.sum(jnp.where(diagonal, tile_row[0:1, :], 0), axis=1, keepdims=True)
    ahead = (owner_col == owner_row) & (lane_i < row_i)
    rank_col = jnp.sum(jnp.where(ahead, 1, 0), axis=1, keepdims=True)
    goes = jnp.where((iota((shards, blocks), 0) == group) & kept, 1.0, 0.0).astype(BF16)
    rows_in = jnp.where(iota((blocks, PIX), 1) == rank_col, (row_col + 1).astype(F32), 0.0)
    meta = dot(goes, rows_in.astype(BF16))
    meta_out[...] = meta
    meta_in[0:1, :] = meta[0:1, :]
    mix = jnp.concatenate(
        [jnp.broadcast_to(mixing[0, :, c : c + 1], (NBEAM, PIX)) for c in range(NCOMP)], axis=0
    )
    mix_out[...] = mix
    mix_in[0] = mix

    for copy in loads[3:]:
        copy.wait()
    lag_table(taps, weights, table)
    for copy in loads_x:
        copy.wait()

    def sums_of(target, block):
        lagged_sums(x, table, target, block, blocks)

    sums_of(even, blocks + STEP)
    sums_of(odd, 0)
    add_diagonals(even, here, before, blocks + STEP)

    def two_chunks(block):
        sums_of(even, block)
        add_diagonals(odd, here, before, block - STEP)
        sums_of(odd, block + STEP)
        add_diagonals(even, here, before, block)

    for i in range(2):
        two_chunks(STEP + 2 * STEP * i)
    overhang[0] = here[0:STEP, :] + before[pl.ds(1, STEP), :]
    overhang[1] = here[pl.ds(blocks + STEP, STEP), :] + before[pl.ds(blocks + STEP + 1, STEP), :]

    pl.semaphore_wait(
        barrier,
        shards
        - 1
        + bands
        - 1
        + jnp.where((band != 0) & has_right, 1, 0)
        + jnp.where((band != bands - 1) & has_left, 1, 0),
    )

    to_left = pltpu.make_async_remote_copy(
        overhang.at[0],
        arrived.at[1],
        halo_send.at[0],
        halo_recv.at[1],
        device_id=(band, left),
        device_id_type=MESH,
    )
    to_right = pltpu.make_async_remote_copy(
        overhang.at[1],
        arrived.at[0],
        halo_send.at[1],
        halo_recv.at[0],
        device_id=(band, right),
        device_id_type=MESH,
    )

    @pl.when(has_right)
    def _():
        to_right.start()

    @pl.when(has_left)
    def _():
        to_left.start()

    def to_shards(source, target, rows, which):
        for i in order:
            pltpu.make_async_remote_copy(
                source.at[pl.ds(rows * i, rows)],
                target.at[pl.ds(rows * i, rows)],
                peer_send.at[which],
                peer_recv.at[which],
                device_id=(band, shard_peer(i)),
                device_id_type=MESH,
            ).start()

    def from_shards(ref, rows, sem):
        part = ref.at[pl.ds(rows, rows * (shards - 1))]
        pltpu.make_async_copy(part, part, sem).wait()

    to_shards(meta_out, meta_in, 1, 0)
    for i in range(1, bands):
        pltpu.make_async_remote_copy(
            mix_out,
            mix_in.at[i],
            band_send.at[0, i],
            band_recv.at[0, i],
            device_id=(lax.rem(band + i, bands), shard),
            device_id_type=MESH,
        ).start()

    for i in range(2, blocks // (2 * STEP)):
        two_chunks(STEP + 2 * STEP * i)
    add_diagonals(odd, here, before, blocks)

    for side_of, exists in enumerate((has_left, has_right)):

        @pl.when(exists)
        def _(side_of=side_of):
            part = arrived.at[side_of]
            pltpu.make_async_copy(part, part, halo_recv.at[side_of]).wait()

        @pl.when(jnp.logical_not(exists))
        def _(side_of=side_of):
            arrived[side_of] = jnp.zeros((STEP, PIX), F32)

    own = here[pl.ds(STEP, blocks), :] + before[pl.ds(STEP + 1, blocks), :]
    block_values = jnp.concatenate(
        [own[0:STEP] + arrived[0], own[STEP : blocks - STEP], own[blocks - STEP :] + arrived[1]],
        axis=0,
    )
    value_high, value_low = split(block_values)
    values = dot(pick, value_high) + dot(pick, value_low)
    vals_out[...] = values
    vals_in[0:CAP, :] = values[0:CAP, :]
    to_shards(vals_out, vals_in, CAP, 1)

    long = span + 2 * REACH
    row_mats = jnp.concatenate(
        [band_rows(beam_rows[0, k : k + 1, :], long, BEAM - 1) for k in range(NBEAM)],
        axis=0,
    )
    rows_high, rows_low = split(row_mats)
    from_shards(meta_in, 1, peer_recv.at[0])
    slot_i, slot_lane = iota((slots, PIX), 0), iota((slots, PIX), 1)
    spread = jnp.where(iota((slots, shards), 0) // CAP == iota((slots, shards), 1), 1.0, 0.0)
    listed = dot(spread.astype(BF16), meta_in[...].astype(BF16))
    row_of = jnp.sum(jnp.where(slot_i % CAP == slot_lane, listed, 0.0), axis=1, keepdims=True)
    hot = jnp.where((slot_lane + 1).astype(F32) == row_of, 1.0, 0.0).astype(BF16)
    slot_high = dot_nt(rows_high, hot).astype(BF16)
    slot_low = dot_nt(rows_low, hot).astype(BF16)
    cols = [split(band_rows(beam_cols[0, k : k + 1, :], PIX, REACH)) for k in range(NBEAM)]

    from_shards(vals_in, CAP, peer_recv.at[1])
    in_high, in_low = split(vals_in[...])
    both = dot(slot_high, jnp.concatenate([in_high, in_low], axis=1))
    rowed = both[:, 0:PIX] + both[:, PIX:] + dot(slot_low, in_high)
    for k in range(NBEAM):
        rowed_high, rowed_low = split(rowed[long * k : long * (k + 1), :])
        both = dot_nt(rowed_high, jnp.concatenate(cols[k], axis=0))
        wide[k] = both[:, 0:PIX] + both[:, PIX:] + dot_nt(rowed_low, cols[k][0])

    below = pltpu.make_async_remote_copy(
        wide.at[:, pl.ds(REACH + span, REACH), :],
        edge.at[lax.rem(bands - band, bands)],
        edge_send.at[0],
        edge_recv.at[lax.rem(bands - band, bands)],
        device_id=(0, right),
        device_id_type=MESH,
    )
    above = pltpu.make_async_remote_copy(
        wide.at[:, pl.ds(0, REACH), :],
        edge.at[bands - 1 - band],
        edge_send.at[1],
        edge_recv.at[bands - 1 - band],
        device_id=(bands - 1, left),
        device_id_type=MESH,
    )

    @pl.when(has_right)
    def _():
        below.start()

    @pl.when(has_left)
    def _():
        above.start()

    sends = []
    for i in range(1, bands):
        peer = lax.rem(band + i, bands)
        copy = pltpu.make_async_remote_copy(
            wide.at[:, pl.ds(pl.multiple_of(REACH + share * peer, REACH), share), :],
            mine.at[i],
            band_send.at[1, i],
            band_recv.at[1, i],
            device_id=(peer, shard),
            device_id_type=MESH,
        )
        copy.start()
        sends.append(copy)
    mine[0] = wide[:, pl.ds(pl.multiple_of(REACH + share * band, REACH), share), :]
    for i in range(1, bands):
        pltpu.make_async_copy(mix_in.at[i], mix_in.at[i], band_recv.at[0, i]).wait()
    for i in range(1, bands):
        pltpu.make_async_copy(mine.at[i], mine.at[i], band_recv.at[1, i]).wait()

    @pl.when(((band == 0) & has_left) | ((band == bands - 1) & has_right))
    def _():
        for i in range(bands):
            pltpu.make_async_copy(edge.at[i], edge.at[i], edge_recv.at[i]).wait()
        mine[...] += edge[...]

    for c in range(NCOMP):
        total = None
        for i in range(bands):
            for k in range(NBEAM):
                term = mix_in[i, c * NBEAM + k : c * NBEAM + k + 1, :] * mine[i, k]
                total = term if total is None else total + term
        out[c, 0] = total

    @pl.when(has_right)
    def _():
        to_right.wait_send()
        below.wait_send()

    @pl.when(has_left)
    def _():
        to_left.wait_send()
        above.wait_send()

    from_shards(meta_out, 1, peer_send.at[0])
    from_shards(vals_out, CAP, peer_send.at[1])
    for i in range(1, bands):
        pltpu.make_async_copy(mix_out, mix_out, band_send.at[0, i]).wait()
    for copy in sends:
        copy.wait_send()


def on_device(
    tod, filter_taps, det_weights, owner, tile_row, block_counts, beam_rows, beam_cols, mixing
):
    bands, shards = lax.axis_size("band"), lax.axis_size("tm")
    side = 8 if shards >= 16 else shards // 2
    det, samples = tod.shape[1:]
    slots = shards * CAP
    long = bands * REACH + 2 * REACH
    blocks = samples // PIX
    vmem = pl.BlockSpec(memory_space=pltpu.VMEM)
    return pl.pallas_call(
        functools.partial(kernel, bands, shards, side),
        out_shape=jax.ShapeDtypeStruct((NCOMP, 1, REACH, PIX), F32),
        in_specs=[pl.BlockSpec(memory_space=pltpu.HBM)] * 8
        + [pl.BlockSpec(memory_space=pltpu.SMEM)],
        out_specs=vmem,
        scratch_shapes=[
            pltpu.VMEM(filter_taps.shape, BF16),
            pltpu.VMEM((1, det), F32),
            pltpu.VMEM((1, blocks), jnp.int32),
            pltpu.VMEM((1, blocks), jnp.int32),
            pltpu.VMEM(beam_rows.shape, F32),
            pltpu.VMEM(beam_cols.shape, F32),
            pltpu.VMEM((1, NBEAM, NCOMP), F32),
            pltpu.VMEM((det, samples + 4 * HALF), BF16),
            pltpu.VMEM((2 * PIX + 16, LAGS * det), BF16),
            pltpu.VMEM((blocks + 3 * STEP, PIX), F32),
            pltpu.VMEM((blocks + 3 * STEP, PIX), F32),
            pltpu.VMEM((2 * PIX + 16, CHUNK), F32),
            pltpu.VMEM((2 * PIX + 16, CHUNK), F32),
            pltpu.VMEM((2, STEP, PIX), F32),
            pltpu.VMEM((2, STEP, PIX), F32),
            pltpu.VMEM((shards, PIX), F32),
            pltpu.VMEM((shards, PIX), F32),
            pltpu.VMEM((slots, PIX), F32),
            pltpu.VMEM((slots, PIX), F32),
            pltpu.VMEM((NCOMP * NBEAM, PIX), F32),
            pltpu.VMEM((bands, NCOMP * NBEAM, PIX), F32),
            pltpu.VMEM((NBEAM, long, PIX), F32),
            pltpu.VMEM((bands, NBEAM, REACH, PIX), F32),
            pltpu.VMEM((bands, NBEAM, REACH, PIX), F32),
            pltpu.SemaphoreType.DMA((PARTS,)),
            pltpu.SemaphoreType.DMA((7,)),
            pltpu.SemaphoreType.DMA((2,)),
            pltpu.SemaphoreType.DMA((2,)),
            pltpu.SemaphoreType.DMA((2,)),
            pltpu.SemaphoreType.DMA((2,)),
            pltpu.SemaphoreType.DMA((2, bands)),
            pltpu.SemaphoreType.DMA((2, bands)),
            pltpu.SemaphoreType.DMA((2,)),
            pltpu.SemaphoreType.DMA((bands,)),
        ],
        compiler_params=pltpu.CompilerParams(
            collective_id=0, has_side_effects=True, vmem_limit_bytes=50331648
        ),
    )(
        *(pltpu.with_memory_space_constraint(v, pltpu.HBM) for v in (tod,
        filter_taps,
        det_weights,
        owner.reshape(1, blocks),
        tile_row,
        beam_rows,
        beam_cols,
        mixing.transpose(1, 2, 0),)),
        block_counts,
    )


def solution(mesh):
    placed = (
        P("band", None, "tm"),
        P("band", None, None),
        P("band", None),
        P("band", "tm", None),
        P("band", "tm"),
        P("band", "tm"),
        P("band", None, None),
        P("band", None, None),
        P(None, "band", None),
    )
    return jax.shard_map(
        on_device,
        mesh=mesh,
        in_specs=placed,
        out_specs=P(None, "tm", "band", None),
        check_vma=False,
    )
```

```python
import functools

import jax
import jax.numpy as jnp
from jax import lax
from jax.experimental import pallas as pl
from jax.experimental.pallas import tpu as pltpu
from jax.sharding import PartitionSpec as P

PIX = 128
CAP = 8
HALF = 1024
LAGS = 16
BEAM = 33
REACH = 16
NBEAM = 2
NCOMP = 4
CHUNK = 1024
PARTS = 4
STEP = CHUNK // PIX
MESH = pl.DeviceIdType.MESH
F32 = jnp.float32
BF16 = jnp.bfloat16
NT = (((1,), (1,)), ((), ()))


def iota(shape, axis):
    return lax.broadcasted_iota(jnp.int32, shape, axis)


def split(value):
    high = value.astype(BF16)
    return high, (value - high.astype(F32)).astype(BF16)


def dot(a, b):
    return jnp.dot(a, b, preferred_element_type=F32)


def dot_nt(a, b):
    return lax.dot_general(a, b, NT, preferred_element_type=F32)


def lag_table(taps, weights, table):
    det = taps.shape[1]
    eye = iota((det, det), 0) == iota((det, det), 1)
    column = jnp.sum(jnp.where(eye, weights[0:1, :], 0.0), axis=1, keepdims=True)
    flip = jnp.where(iota((PIX, PIX), 0) + iota((PIX, PIX), 1) == PIX - 1, 1.0, 0.0).astype(BF16)
    pair = 2 * PIX
    for j in range(LAGS // 2):
        both = jnp.concatenate(
            [taps[0, :, pl.ds(pair * j + PIX * e, PIX)].astype(F32) * column for e in range(2)],
            axis=0,
        )
        turned = dot_nt(flip, jnp.concatenate(split(both), axis=0)).astype(BF16)
        lanes = pl.ds(2 * det * j, 2 * det)
        table[0:PIX, lanes] = turned[:, 0 : 2 * det]
        table[PIX : 2 * PIX, lanes] = turned[:, 2 * det :]
    last = taps[0, :, 2 * HALF : 2 * HALF + 1].astype(F32) * column
    last_high = last.astype(BF16).astype(F32)
    spot = iota((det, 2 * det), 1) == iota((det, 2 * det), 0) + det
    row_high = jnp.sum(jnp.where(spot, last_high, 0.0), axis=0, keepdims=True)
    row_low = jnp.sum(jnp.where(spot, last - last_high, 0.0), axis=0, keepdims=True)
    rows = iota((16, 2 * det), 0)
    rest = (LAGS - 2) * det
    table[2 * PIX : 2 * PIX + 16, 0:rest] = jnp.zeros((16, rest), BF16)
    table[2 * PIX : 2 * PIX + 16, rest : rest + 2 * det] = jnp.where(
        rows == 0, row_high, jnp.where(rows == 1, row_low, 0.0)
    ).astype(BF16)


def lagged_sums(x, table, sums, block, blocks):
    det = x.shape[0]
    top = 2 * PIX
    for piece in range(2):
        first = block + piece * STEP // 2
        lanes = pl.ds(piece * CHUNK // 2, CHUNK // 2)
        total = last = None
        for q in (3, 2, 1, 0):
            if first + STEP // 2 + 4 * q + 3 <= LAGS or first + 4 * q >= blocks + LAGS:
                continue
            window = jnp.concatenate(
                [x[:, pl.ds(PIX * (first + 4 * q + e), CHUNK // 2)] for e in range(4)], axis=0
            )
            rows = top + 16 if q == 3 else top
            part = dot(table[0:rows, 4 * det * q : 4 * det * (q + 1)], window)
            if q == 3:
                last = part[top:]
            total = part[0:top] if total is None else total + part[0:top]
        shape = (top, CHUNK // 2)
        sums[0:top, lanes] = jnp.zeros(shape, F32) if total is None else total
        sums[pl.ds(top, 16), lanes] = jnp.zeros((16, CHUNK // 2), F32) if last is None else last


def add_diagonals(sums, here, before, block):
    keeps = iota((PIX, PIX), 1) <= iota((PIX, PIX), 0)
    prior = None
    for k in range(STEP):
        lanes = pl.ds(PIX * k, PIX)
        turned = pltpu.roll(
            sums[0:PIX, lanes] + sums[PIX : 2 * PIX, lanes], 1, 1, stride=1, stride_axis=0
        )
        final = sums[2 * PIX : 2 * PIX + 1, lanes] + sums[2 * PIX + 1 : 2 * PIX + 2, lanes]
        merged = jnp.where(keeps, 0.0 if k == 0 else prior, turned)
        done = jnp.sum(merged, axis=0, keepdims=True) + final
        if k == 0:
            before[pl.ds(block, 1), :] = done
        else:
            here[pl.ds(block + k - 1, 1), :] = done
        prior = turned
    here[pl.ds(block + STEP - 1, 1), :] = jnp.sum(
        jnp.where(keeps, prior, 0.0), axis=0, keepdims=True
    )


def band_rows(profile, out_rows, shift):
    wide = jnp.concatenate([profile, jnp.zeros((1, PIX - BEAM), F32)], axis=1)
    spread = jnp.broadcast_to(wide, (out_rows, PIX))
    turned = pltpu.roll(spread, PIX - shift, 1, stride=1, stride_axis=0)
    tap = iota((out_rows, PIX), 1) - iota((out_rows, PIX), 0) + shift
    return jnp.where((tap >= 0) & (tap < BEAM), turned, 0.0)


def kernel(
    bands,
    shards,
    side,
    tod,
    taps_hbm,
    weights_hbm,
    owner_hbm,
    tile_row_hbm,
    beam_rows_hbm,
    beam_cols_hbm,
    mixing_hbm,
    counts,
    out,
    taps,
    weights,
    owner,
    tile_row,
    beam_rows,
    beam_cols,
    mixing,
    x,
    table,
    here,
    before,
    even,
    odd,
    overhang,
    arrived,
    meta_out,
    meta_in,
    vals_out,
    vals_in,
    mix_out,
    mix_in,
    wide,
    mine,
    edge,
    load_sem,
    small_sem,
    halo_send,
    halo_recv,
    peer_send,
    peer_recv,
    band_send,
    band_recv,
    edge_send,
    edge_recv,
):
    band = lax.axis_index("band")
    shard = lax.axis_index("tm")
    depth = shards // side
    sx, sz = lax.div(shard, side), lax.rem(shard, side)
    samples = tod.shape[2]
    blocks = samples // PIX
    share = REACH
    span = bands * share
    has_left, has_right = shard > 0, shard < shards - 1
    left, right = lax.rem(shard + shards - 1, shards), lax.rem(shard + 1, shards)

    def shard_peer(i):
        return lax.rem(sx + i // side, depth) * side + lax.rem(sz + i % side, side)

    def hops(i):
        dx, dz = i // side, i % side
        return min(dx, depth - dx) + min(dz, side - dz)

    loads = []
    for n, (source, target) in enumerate(
        (
            (taps_hbm, taps),
            (weights_hbm, weights),
            (owner_hbm, owner),
            (tile_row_hbm, tile_row),
            (mixing_hbm, mixing),
            (beam_rows_hbm, beam_rows),
            (beam_cols_hbm, beam_cols),
        )
    ):
        loads.append(pltpu.make_async_copy(source, target, small_sem.at[n]))
        loads[-1].start()
    loads_x = []
    for n in range(PARTS):
        rows = pl.ds(n * tod.shape[1] // PARTS, tod.shape[1] // PARTS)
        loads_x.append(
            pltpu.make_async_copy(
                tod.at[0, rows], x.at[rows, pl.ds(2 * HALF, samples)], load_sem.at[n]
            )
        )
        loads_x[-1].start()

    order = sorted(range(1, shards), key=lambda i: -hops(i))

    barrier = pltpu.get_barrier_semaphore()
    for i in order:
        pl.semaphore_signal(barrier, 1, device_id=(band, shard_peer(i)), device_id_type=MESH)
    for i in range(1, bands):
        pl.semaphore_signal(barrier, 1, device_id=(lax.rem(band + i, bands), shard), device_id_type=MESH)

    @pl.when((band == 0) & has_left)
    def _():
        for b in range(1, bands):
            pl.semaphore_signal(barrier, 1, device_id=(b, left), device_id_type=MESH)

    @pl.when((band == bands - 1) & has_right)
    def _():
        for b in range(bands - 1):
            pl.semaphore_signal(barrier, 1, device_id=(b, right), device_id_type=MESH)

    before[...] = jnp.zeros_like(before)
    for start in (0, samples + 2 * HALF):
        x[:, pl.ds(start, 2 * HALF)] = jnp.zeros((x.shape[0], 2 * HALF), BF16)

    for copy in loads[:2]:
        copy.wait()
    lag_table(taps, weights, table)
    for copy in loads[2:] + loads_x:
        copy.wait()

    row_i, lane_i = iota((blocks, blocks), 0), iota((blocks, blocks), 1)
    diagonal = row_i == lane_i
    owner_row = owner[0:1, :]
    owner_col = jnp.sum(jnp.where(diagonal, owner_row, 0), axis=1, keepdims=True)
    same = (owner_col == owner_row) & (row_i < lane_i)
    rank_row = jnp.sum(jnp.where(same, 1, 0), axis=0, keepdims=True)
    ox, oz = owner_row // side, owner_row % side
    group = ((ox - sx + depth) % depth) * side + (oz - sz + side) % side
    slot_row = group * CAP + rank_row
    kept = iota((1, blocks), 1) < counts[0, 0]
    slots = shards * CAP
    pick = jnp.where((iota((slots, blocks), 0) == slot_row) & kept, 1.0, 0.0).astype(BF16)
    row_col = jnp.sum(jnp.where(diagonal, tile_row[0:1, :], 0), axis=1, keepdims=True)
    ahead = (owner_col == owner_row) & (lane_i < row_i)
    rank_col = jnp.sum(jnp.where(ahead, 1, 0), axis=1, keepdims=True)
    goes = jnp.where((iota((shards, blocks), 0) == group) & kept, 1.0, 0.0).astype(BF16)
    rows_in = jnp.where(iota((blocks, PIX), 1) == rank_col, (row_col + 1).astype(F32), 0.0)
    meta = dot(goes, rows_in.astype(BF16))
    meta_out[...] = meta
    meta_in[0:1, :] = meta[0:1, :]
    mix = jnp.concatenate(
        [jnp.broadcast_to(mixing[0, :, c : c + 1], (NBEAM, PIX)) for c in range(NCOMP)], axis=0
    )
    mix_out[...] = mix
    mix_in[0] = mix

    def sums_of(target, block):
        lagged_sums(x, table, target, block, blocks)

    sums_of(even, blocks + STEP)
    sums_of(odd, 0)
    add_diagonals(even, here, before, blocks + STEP)

    def two_chunks(block):
        sums_of(even, block)
        add_diagonals(odd, here, before, block - STEP)
        sums_of(odd, block + STEP)
        add_diagonals(even, here, before, block)

    for i in range(2):
        two_chunks(STEP + 2 * STEP * i)
    overhang[0] = here[0:STEP, :] + before[pl.ds(1, STEP), :]
    overhang[1] = here[pl.ds(blocks + STEP, STEP), :] + before[pl.ds(blocks + STEP + 1, STEP), :]

    pl.semaphore_wait(
        barrier,
        shards
        - 1
        + bands
        - 1
        + jnp.where((band != 0) & has_right, 1, 0)
        + jnp.where((band != bands - 1) & has_left, 1, 0),
    )

    to_left = pltpu.make_async_remote_copy(
        overhang.at[0],
        arrived.at[1],
        halo_send.at[0],
        halo_recv.at[1],
        device_id=(band, left),
        device_id_type=MESH,
    )
    to_right = pltpu.make_async_remote_copy(
        overhang.at[1],
        arrived.at[0],
        halo_send.at[1],
        halo_recv.at[0],
        device_id=(band, right),
        device_id_type=MESH,
    )

    @pl.when(has_right)
    def _():
        to_right.start()

    @pl.when(has_left)
    def _():
        to_left.start()

    def to_shards(source, target, rows, which):
        for i in order:
            pltpu.make_async_remote_copy(
                source.at[pl.ds(rows * i, rows)],
                target.at[pl.ds(rows * i, rows)],
                peer_send.at[which],
                peer_recv.at[which],
                device_id=(band, shard_peer(i)),
                device_id_type=MESH,
            ).start()

    def from_shards(ref, rows, sem):
        part = ref.at[pl.ds(rows, rows * (shards - 1))]
        pltpu.make_async_copy(part, part, sem).wait()

    to_shards(meta_out, meta_in, 1, 0)
    for i in range(1, bands):
        pltpu.make_async_remote_copy(
            mix_out,
            mix_in.at[i],
            band_send.at[0, i],
            band_recv.at[0, i],
            device_id=(lax.rem(band + i, bands), shard),
            device_id_type=MESH,
        ).start()

    for i in range(2, blocks // (2 * STEP)):
        two_chunks(STEP + 2 * STEP * i)
    add_diagonals(odd, here, before, blocks)

    for side_of, exists in enumerate((has_left, has_right)):

        @pl.when(exists)
        def _(side_of=side_of):
            part = arrived.at[side_of]
            pltpu.make_async_copy(part, part, halo_recv.at[side_of]).wait()

        @pl.when(jnp.logical_not(exists))
        def _(side_of=side_of):
            arrived[side_of] = jnp.zeros((STEP, PIX), F32)

    own = here[pl.ds(STEP, blocks), :] + before[pl.ds(STEP + 1, blocks), :]
    block_values = jnp.concatenate(
        [own[0:STEP] + arrived[0], own[STEP : blocks - STEP], own[blocks - STEP :] + arrived[1]],
        axis=0,
    )
    value_high, value_low = split(block_values)
    both = dot(pick, jnp.concatenate([value_high, value_low], axis=1))
    values = both[:, 0:PIX] + both[:, PIX:]
    vals_out[...] = values
    vals_in[0:CAP, :] = values[0:CAP, :]
    to_shards(vals_out, vals_in, CAP, 1)

    long = span + 2 * REACH
    row_mats = jnp.concatenate(
        [band_rows(beam_rows[0, k : k + 1, :], long, BEAM - 1) for k in range(NBEAM)],
        axis=0,
    )
    rows_high, rows_low = split(row_mats)
    from_shards(meta_in, 1, peer_recv.at[0])
    slot_i, slot_lane = iota((slots, PIX), 0), iota((slots, PIX), 1)
    spread = jnp.where(iota((slots, shards), 0) // CAP == iota((slots, shards), 1), 1.0, 0.0)
    listed = dot(spread.astype(BF16), meta_in[...].astype(BF16))
    row_of = jnp.sum(jnp.where(slot_i % CAP == slot_lane, listed, 0.0), axis=1, keepdims=True)
    hot = jnp.where((slot_lane + 1).astype(F32) == row_of, 1.0, 0.0).astype(BF16)
    slot_high = dot_nt(rows_high, hot).astype(BF16)
    slot_low = dot_nt(rows_low, hot).astype(BF16)
    cols = [split(band_rows(beam_cols[0, k : k + 1, :], PIX, REACH)) for k in range(NBEAM)]

    from_shards(vals_in, CAP, peer_recv.at[1])
    in_high, in_low = split(vals_in[...])
    both = dot(slot_high, jnp.concatenate([in_high, in_low], axis=1))
    rowed = both[:, 0:PIX] + both[:, PIX:] + dot(slot_low, in_high)
    for k in range(NBEAM):
        rowed_high, rowed_low = split(rowed[long * k : long * (k + 1), :])
        both = dot_nt(rowed_high, jnp.concatenate(cols[k], axis=0))
        wide[k] = both[:, 0:PIX] + both[:, PIX:] + dot_nt(rowed_low, cols[k][0])

    below = pltpu.make_async_remote_copy(
        wide.at[:, pl.ds(REACH + span, REACH), :],
        edge.at[lax.rem(bands - band, bands)],
        edge_send.at[0],
        edge_recv.at[lax.rem(bands - band, bands)],
        device_id=(0, right),
        device_id_type=MESH,
    )
    above = pltpu.make_async_remote_copy(
        wide.at[:, pl.ds(0, REACH), :],
        edge.at[bands - 1 - band],
        edge_send.at[1],
        edge_recv.at[bands - 1 - band],
        device_id=(bands - 1, left),
        device_id_type=MESH,
    )

    @pl.when(has_right)
    def _():
        below.start()

    @pl.when(has_left)
    def _():
        above.start()

    sends = []
    for i in sorted(range(1, bands), key=lambda i: -min(i, bands - i)):
        peer = lax.rem(band + i, bands)
        copy = pltpu.make_async_remote_copy(
            wide.at[:, pl.ds(pl.multiple_of(REACH + share * peer, REACH), share), :],
            mine.at[i],
            band_send.at[1, i],
            band_recv.at[1, i],
            device_id=(peer, shard),
            device_id_type=MESH,
        )
        copy.start()
        sends.append(copy)
    mine[0] = wide[:, pl.ds(pl.multiple_of(REACH + share * band, REACH), share), :]
    for i in range(1, bands):
        pltpu.make_async_copy(mix_in.at[i], mix_in.at[i], band_recv.at[0, i]).wait()
    for i in range(1, bands):
        pltpu.make_async_copy(mine.at[i], mine.at[i], band_recv.at[1, i]).wait()

    @pl.when(((band == 0) & has_left) | ((band == bands - 1) & has_right))
    def _():
        for i in range(bands):
            pltpu.make_async_copy(edge.at[i], edge.at[i], edge_recv.at[i]).wait()
        mine[...] += edge[...]

    for c in range(NCOMP):
        total = None
        for i in range(bands):
            for k in range(NBEAM):
                term = mix_in[i, c * NBEAM + k : c * NBEAM + k + 1, :] * mine[i, k]
                total = term if total is None else total + term
        out[c, 0] = total

    @pl.when(has_right)
    def _():
        to_right.wait_send()
        below.wait_send()

    @pl.when(has_left)
    def _():
        to_left.wait_send()
        above.wait_send()

    from_shards(meta_out, 1, peer_send.at[0])
    from_shards(vals_out, CAP, peer_send.at[1])
    for i in range(1, bands):
        pltpu.make_async_copy(mix_out, mix_out, band_send.at[0, i]).wait()
    for copy in sends:
        copy.wait_send()


def on_device(
    tod, filter_taps, det_weights, owner, tile_row, block_counts, beam_rows, beam_cols, mixing
):
    bands, shards = lax.axis_size("band"), lax.axis_size("tm")
    side = 8 if shards >= 16 else shards // 2
    det, samples = tod.shape[1:]
    slots = shards * CAP
    long = bands * REACH + 2 * REACH
    blocks = samples // PIX
    vmem = pl.BlockSpec(memory_space=pltpu.VMEM)
    return pl.pallas_call(
        functools.partial(kernel, bands, shards, side),
        out_shape=jax.ShapeDtypeStruct((NCOMP, 1, REACH, PIX), F32),
        in_specs=[pl.BlockSpec(memory_space=pltpu.HBM)] * 8
        + [pl.BlockSpec(memory_space=pltpu.SMEM)],
        out_specs=vmem,
        scratch_shapes=[
            pltpu.VMEM(filter_taps.shape, BF16),
            pltpu.VMEM((1, det), F32),
            pltpu.VMEM((1, blocks), jnp.int32),
            pltpu.VMEM((1, blocks), jnp.int32),
            pltpu.VMEM(beam_rows.shape, F32),
            pltpu.VMEM(beam_cols.shape, F32),
            pltpu.VMEM((1, NBEAM, NCOMP), F32),
            pltpu.VMEM((det, samples + 4 * HALF), BF16),
            pltpu.VMEM((2 * PIX + 16, LAGS * det), BF16),
            pltpu.VMEM((blocks + 3 * STEP, PIX), F32),
            pltpu.VMEM((blocks + 3 * STEP, PIX), F32),
            pltpu.VMEM((2 * PIX + 16, CHUNK), F32),
            pltpu.VMEM((2 * PIX + 16, CHUNK), F32),
            pltpu.VMEM((2, STEP, PIX), F32),
            pltpu.VMEM((2, STEP, PIX), F32),
            pltpu.VMEM((shards, PIX), F32),
            pltpu.VMEM((shards, PIX), F32),
            pltpu.VMEM((slots, PIX), F32),
            pltpu.VMEM((slots, PIX), F32),
            pltpu.VMEM((NCOMP * NBEAM, PIX), F32),
            pltpu.VMEM((bands, NCOMP * NBEAM, PIX), F32),
            pltpu.VMEM((NBEAM, long, PIX), F32),
            pltpu.VMEM((bands, NBEAM, REACH, PIX), F32),
            pltpu.VMEM((bands, NBEAM, REACH, PIX), F32),
            pltpu.SemaphoreType.DMA((PARTS,)),
            pltpu.SemaphoreType.DMA((7,)),
            pltpu.SemaphoreType.DMA((2,)),
            pltpu.SemaphoreType.DMA((2,)),
            pltpu.SemaphoreType.DMA((2,)),
            pltpu.SemaphoreType.DMA((2,)),
            pltpu.SemaphoreType.DMA((2, bands)),
            pltpu.SemaphoreType.DMA((2, bands)),
            pltpu.SemaphoreType.DMA((2,)),
            pltpu.SemaphoreType.DMA((bands,)),
        ],
        compiler_params=pltpu.CompilerParams(
            collective_id=0, has_side_effects=True, vmem_limit_bytes=50331648
        ),
    )(
        *(pltpu.with_memory_space_constraint(v, pltpu.HBM) for v in (tod,
        filter_taps,
        det_weights,
        owner.reshape(1, blocks),
        tile_row,
        beam_rows,
        beam_cols,
        mixing.transpose(1, 2, 0),)),
        block_counts,
    )


def solution(mesh):
    placed = (
        P("band", None, "tm"),
        P("band", None, None),
        P("band", None),
        P("band", "tm", None),
        P("band", "tm"),
        P("band", "tm"),
        P("band", None, None),
        P("band", None, None),
        P(None, "band", None),
    )
    return jax.shard_map(
        on_device,
        mesh=mesh,
        in_specs=placed,
        out_specs=P(None, "tm", "band", None),
        check_vma=False,
    )
```

```python
import functools

import jax
import jax.numpy as jnp
from jax import lax
from jax.experimental import pallas as pl
from jax.experimental.pallas import tpu as pltpu
from jax.sharding import PartitionSpec as P

PIX = 128
CAP = 8
HALF = 1024
LAGS = 16
BEAM = 33
REACH = 16
NBEAM = 2
NCOMP = 4
CHUNK = 1024
PARTS = 4
STEP = CHUNK // PIX
MESH = pl.DeviceIdType.MESH
F32 = jnp.float32
BF16 = jnp.bfloat16
NT = (((1,), (1,)), ((), ()))


def iota(shape, axis):
    return lax.broadcasted_iota(jnp.int32, shape, axis)


def split(value):
    high = value.astype(BF16)
    return high, (value - high.astype(F32)).astype(BF16)


def dot(a, b):
    return jnp.dot(a, b, preferred_element_type=F32)


def dot_nt(a, b):
    return lax.dot_general(a, b, NT, preferred_element_type=F32)


def lag_table(taps, weights, table):
    det = taps.shape[1]
    eye = iota((det, det), 0) == iota((det, det), 1)
    column = jnp.sum(jnp.where(eye, weights[0:1, :], 0.0), axis=1, keepdims=True)
    flip = jnp.where(iota((PIX, PIX), 0) + iota((PIX, PIX), 1) == PIX - 1, 1.0, 0.0).astype(BF16)
    pair = 2 * PIX
    for j in range(LAGS // 2):
        both = jnp.concatenate(
            [taps[0, :, pl.ds(pair * j + PIX * e, PIX)].astype(F32) * column for e in range(2)],
            axis=0,
        )
        turned = dot_nt(flip, jnp.concatenate(split(both), axis=0)).astype(BF16)
        lanes = pl.ds(2 * det * j, 2 * det)
        table[0:PIX, lanes] = turned[:, 0 : 2 * det]
        table[PIX : 2 * PIX, lanes] = turned[:, 2 * det :]
    last = taps[0, :, 2 * HALF : 2 * HALF + 1].astype(F32) * column
    last_high = last.astype(BF16).astype(F32)
    spot = iota((det, 2 * det), 1) == iota((det, 2 * det), 0) + det
    row_high = jnp.sum(jnp.where(spot, last_high, 0.0), axis=0, keepdims=True)
    row_low = jnp.sum(jnp.where(spot, last - last_high, 0.0), axis=0, keepdims=True)
    rows = iota((16, 2 * det), 0)
    rest = (LAGS - 2) * det
    table[2 * PIX : 2 * PIX + 16, 0:rest] = jnp.zeros((16, rest), BF16)
    table[2 * PIX : 2 * PIX + 16, rest : rest + 2 * det] = jnp.where(
        rows == 0, row_high, jnp.where(rows == 1, row_low, 0.0)
    ).astype(BF16)


def lagged_sums(x, table, sums, block, blocks):
    det = x.shape[0]
    top = 2 * PIX
    for piece in range(2):
        first = block + piece * STEP // 2
        lanes = pl.ds(piece * CHUNK // 2, CHUNK // 2)
        total = last = None
        for q in (3, 2, 1, 0):
            if first + STEP // 2 + 4 * q + 3 <= LAGS or first + 4 * q >= blocks + LAGS:
                continue
            window = jnp.concatenate(
                [x[:, pl.ds(PIX * (first + 4 * q + e), CHUNK // 2)] for e in range(4)], axis=0
            )
            rows = top + 16 if q == 3 else top
            part = dot(table[0:rows, 4 * det * q : 4 * det * (q + 1)], window)
            if q == 3:
                last = part[top:]
            total = part[0:top] if total is None else total + part[0:top]
        shape = (top, CHUNK // 2)
        sums[0:top, lanes] = jnp.zeros(shape, F32) if total is None else total
        sums[pl.ds(top, 16), lanes] = jnp.zeros((16, CHUNK // 2), F32) if last is None else last


def add_diagonals(sums, here, before, block):
    keeps = iota((PIX, PIX), 1) <= iota((PIX, PIX), 0)
    prior = None
    for k in range(STEP):
        lanes = pl.ds(PIX * k, PIX)
        turned = pltpu.roll(
            sums[0:PIX, lanes] + sums[PIX : 2 * PIX, lanes], 1, 1, stride=1, stride_axis=0
        )
        final = sums[2 * PIX : 2 * PIX + 1, lanes] + sums[2 * PIX + 1 : 2 * PIX + 2, lanes]
        merged = jnp.where(keeps, 0.0 if k == 0 else prior, turned)
        done = jnp.sum(merged, axis=0, keepdims=True) + final
        if k == 0:
            before[pl.ds(block, 1), :] = done
        else:
            here[pl.ds(block + k - 1, 1), :] = done
        prior = turned
    here[pl.ds(block + STEP - 1, 1), :] = jnp.sum(
        jnp.where(keeps, prior, 0.0), axis=0, keepdims=True
    )


def band_rows(profile, out_rows, shift):
    wide = jnp.concatenate([profile, jnp.zeros((1, PIX - BEAM), F32)], axis=1)
    spread = jnp.broadcast_to(wide, (out_rows, PIX))
    turned = pltpu.roll(spread, PIX - shift, 1, stride=1, stride_axis=0)
    tap = iota((out_rows, PIX), 1) - iota((out_rows, PIX), 0) + shift
    return jnp.where((tap >= 0) & (tap < BEAM), turned, 0.0)


def kernel(
    bands,
    shards,
    side,
    tod,
    taps_hbm,
    weights_hbm,
    owner_hbm,
    tile_row_hbm,
    beam_rows_hbm,
    beam_cols_hbm,
    mixing_hbm,
    counts,
    out,
    taps,
    weights,
    owner,
    tile_row,
    beam_rows,
    beam_cols,
    mixing,
    x,
    table,
    here,
    before,
    even,
    odd,
    overhang,
    arrived,
    meta_out,
    meta_in,
    vals_out,
    vals_in,
    mix_out,
    mix_in,
    wide,
    mine,
    edge,
    load_sem,
    small_sem,
    halo_send,
    halo_recv,
    peer_send,
    peer_recv,
    band_send,
    band_recv,
    edge_send,
    edge_recv,
):
    band = lax.axis_index("band")
    shard = lax.axis_index("tm")
    depth = shards // side
    sx, sz = lax.div(shard, side), lax.rem(shard, side)
    samples = tod.shape[2]
    blocks = samples // PIX
    share = REACH
    span = bands * share
    has_left, has_right = shard > 0, shard < shards - 1
    left, right = lax.rem(shard + shards - 1, shards), lax.rem(shard + 1, shards)

    def shard_peer(i):
        return lax.rem(sx + i // side, depth) * side + lax.rem(sz + i % side, side)

    def hops(i):
        dx, dz = i // side, i % side
        return min(dx, depth - dx) + min(dz, side - dz)

    loads = []
    for n, (source, target) in enumerate(
        (
            (taps_hbm, taps),
            (weights_hbm, weights),
            (owner_hbm, owner),
            (tile_row_hbm, tile_row),
            (mixing_hbm, mixing),
            (beam_rows_hbm, beam_rows),
            (beam_cols_hbm, beam_cols),
        )
    ):
        loads.append(pltpu.make_async_copy(source, target, small_sem.at[n]))
        loads[-1].start()
    loads_x = []
    for n in range(PARTS):
        rows = pl.ds(n * tod.shape[1] // PARTS, tod.shape[1] // PARTS)
        loads_x.append(
            pltpu.make_async_copy(
                tod.at[0, rows], x.at[rows, pl.ds(2 * HALF, samples)], load_sem.at[n]
            )
        )
        loads_x[-1].start()

    order = sorted(range(1, shards), key=lambda i: -hops(i))

    barrier = pltpu.get_barrier_semaphore()
    for i in order:
        pl.semaphore_signal(barrier, 1, device_id=(band, shard_peer(i)), device_id_type=MESH)
    for i in range(1, bands):
        pl.semaphore_signal(barrier, 1, device_id=(lax.rem(band + i, bands), shard), device_id_type=MESH)

    @pl.when((band == 0) & has_left)
    def _():
        for b in range(1, bands):
            pl.semaphore_signal(barrier, 1, device_id=(b, left), device_id_type=MESH)

    @pl.when((band == bands - 1) & has_right)
    def _():
        for b in range(bands - 1):
            pl.semaphore_signal(barrier, 1, device_id=(b, right), device_id_type=MESH)

    before[...] = jnp.zeros_like(before)
    for start in (0, samples + 2 * HALF):
        x[:, pl.ds(start, 2 * HALF)] = jnp.zeros((x.shape[0], 2 * HALF), BF16)

    for copy in loads[:2]:
        copy.wait()
    lag_table(taps, weights, table)
    for copy in loads[2:] + loads_x:
        copy.wait()

    row_i, lane_i = iota((blocks, blocks), 0), iota((blocks, blocks), 1)
    diagonal = row_i == lane_i
    owner_row = owner[0:1, :]
    owner_col = jnp.sum(jnp.where(diagonal, owner_row, 0), axis=1, keepdims=True)
    same = (owner_col == owner_row) & (row_i < lane_i)
    rank_row = jnp.sum(jnp.where(same, 1, 0), axis=0, keepdims=True)
    ox, oz = owner_row // side, owner_row % side
    group = ((ox - sx + depth) % depth) * side + (oz - sz + side) % side
    slot_row = group * CAP + rank_row
    kept = iota((1, blocks), 1) < counts[0, 0]
    slots = shards * CAP
    pick = jnp.where((iota((slots, blocks), 0) == slot_row) & kept, 1.0, 0.0).astype(BF16)
    row_col = jnp.sum(jnp.where(diagonal, tile_row[0:1, :], 0), axis=1, keepdims=True)
    ahead = (owner_col == owner_row) & (lane_i < row_i)
    rank_col = jnp.sum(jnp.where(ahead, 1, 0), axis=1, keepdims=True)
    goes = jnp.where((iota((shards, blocks), 0) == group) & kept, 1.0, 0.0).astype(BF16)
    rows_in = jnp.where(iota((blocks, PIX), 1) == rank_col, (row_col + 1).astype(F32), 0.0)
    meta = dot(goes, rows_in.astype(BF16))
    meta_out[...] = meta
    meta_in[0:1, :] = meta[0:1, :]
    mix = jnp.concatenate(
        [jnp.broadcast_to(mixing[0, :, c : c + 1], (NBEAM, PIX)) for c in range(NCOMP)], axis=0
    )
    mix_out[...] = mix
    mix_in[0] = mix

    def sums_of(target, block):
        lagged_sums(x, table, target, block, blocks)

    sums_of(even, blocks + STEP)
    sums_of(odd, 0)
    add_diagonals(even, here, before, blocks + STEP)

    def two_chunks(block):
        sums_of(even, block)
        add_diagonals(odd, here, before, block - STEP)
        sums_of(odd, block + STEP)
        add_diagonals(even, here, before, block)

    for i in range(2):
        two_chunks(STEP + 2 * STEP * i)
    overhang[0] = here[0:STEP, :] + before[pl.ds(1, STEP), :]
    overhang[1] = here[pl.ds(blocks + STEP, STEP), :] + before[pl.ds(blocks + STEP + 1, STEP), :]

    pl.semaphore_wait(
        barrier,
        shards
        - 1
        + bands
        - 1
        + jnp.where((band != 0) & has_right, 1, 0)
        + jnp.where((band != bands - 1) & has_left, 1, 0),
    )

    to_left = pltpu.make_async_remote_copy(
        overhang.at[0],
        arrived.at[1],
        halo_send.at[0],
        halo_recv.at[1],
        device_id=(band, left),
        device_id_type=MESH,
    )
    to_right = pltpu.make_async_remote_copy(
        overhang.at[1],
        arrived.at[0],
        halo_send.at[1],
        halo_recv.at[0],
        device_id=(band, right),
        device_id_type=MESH,
    )

    @pl.when(has_right)
    def _():
        to_right.start()

    @pl.when(has_left)
    def _():
        to_left.start()

    def to_shards(source, target, rows, which, peers):
        for i in peers:
            pltpu.make_async_remote_copy(
                source.at[pl.ds(rows * i, rows)],
                target.at[pl.ds(rows * i, rows)],
                peer_send.at[which],
                peer_recv.at[which],
                device_id=(band, shard_peer(i)),
                device_id_type=MESH,
            ).start()

    def from_shards(ref, rows, sem):
        part = ref.at[pl.ds(rows, rows * (shards - 1))]
        pltpu.make_async_copy(part, part, sem).wait()

    to_shards(meta_out, meta_in, 1, 0, order)
    for i in range(1, bands):
        pltpu.make_async_remote_copy(
            mix_out,
            mix_in.at[i],
            band_send.at[0, i],
            band_recv.at[0, i],
            device_id=(lax.rem(band + i, bands), shard),
            device_id_type=MESH,
        ).start()

    for i in range(2, blocks // (2 * STEP)):
        two_chunks(STEP + 2 * STEP * i)
    add_diagonals(odd, here, before, blocks)

    for side_of, exists in enumerate((has_left, has_right)):

        @pl.when(exists)
        def _(side_of=side_of):
            part = arrived.at[side_of]
            pltpu.make_async_copy(part, part, halo_recv.at[side_of]).wait()

        @pl.when(jnp.logical_not(exists))
        def _(side_of=side_of):
            arrived[side_of] = jnp.zeros((STEP, PIX), F32)

    own = here[pl.ds(STEP, blocks), :] + before[pl.ds(STEP + 1, blocks), :]
    block_values = jnp.concatenate(
        [own[0:STEP] + arrived[0], own[STEP : blocks - STEP], own[blocks - STEP :] + arrived[1]],
        axis=0,
    )
    value_high, value_low = split(block_values)
    packed = jnp.concatenate([value_high, value_low], axis=1)

    def fill(first, count):
        both = dot(pick[first : first + count], packed)
        values = both[:, 0:PIX] + both[:, PIX:]
        vals_out[pl.ds(first, count), :] = values
        return values

    quarter = slots // 4
    early = [i for i in order if quarter <= i * CAP < 3 * quarter and hops(i) >= 4]
    fill(quarter, 2 * quarter)
    to_shards(vals_out, vals_in, CAP, 1, early)
    vals_in[0:CAP, :] = fill(0, quarter)[0:CAP, :]
    fill(3 * quarter, quarter)
    to_shards(vals_out, vals_in, CAP, 1, [i for i in order if i not in early])

    long = span + 2 * REACH
    row_mats = jnp.concatenate(
        [band_rows(beam_rows[0, k : k + 1, :], long, BEAM - 1) for k in range(NBEAM)],
        axis=0,
    )
    rows_high, rows_low = split(row_mats)
    from_shards(meta_in, 1, peer_recv.at[0])
    slot_i, slot_lane = iota((slots, PIX), 0), iota((slots, PIX), 1)
    spread = jnp.where(iota((slots, shards), 0) // CAP == iota((slots, shards), 1), 1.0, 0.0)
    listed = dot(spread.astype(BF16), meta_in[...].astype(BF16))
    row_of = jnp.sum(jnp.where(slot_i % CAP == slot_lane, listed, 0.0), axis=1, keepdims=True)
    hot = jnp.where((slot_lane + 1).astype(F32) == row_of, 1.0, 0.0).astype(BF16)
    slot_high = dot_nt(rows_high, hot).astype(BF16)
    slot_low = dot_nt(rows_low, hot).astype(BF16)
    cols = [split(band_rows(beam_cols[0, k : k + 1, :], PIX, REACH)) for k in range(NBEAM)]

    from_shards(vals_in, CAP, peer_recv.at[1])
    in_high, in_low = split(vals_in[...])
    both = dot(slot_high, jnp.concatenate([in_high, in_low], axis=1))
    rowed = both[:, 0:PIX] + both[:, PIX:] + dot(slot_low, in_high)
    for k in range(NBEAM):
        rowed_high, rowed_low = split(rowed[long * k : long * (k + 1), :])
        both = dot_nt(rowed_high, jnp.concatenate(cols[k], axis=0))
        wide[k] = both[:, 0:PIX] + both[:, PIX:] + dot_nt(rowed_low, cols[k][0])

    below = pltpu.make_async_remote_copy(
        wide.at[:, pl.ds(REACH + span, REACH), :],
        edge.at[lax.rem(bands - band, bands)],
        edge_send.at[0],
        edge_recv.at[lax.rem(bands - band, bands)],
        device_id=(0, right),
        device_id_type=MESH,
    )
    above = pltpu.make_async_remote_copy(
        wide.at[:, pl.ds(0, REACH), :],
        edge.at[bands - 1 - band],
        edge_send.at[1],
        edge_recv.at[bands - 1 - band],
        device_id=(bands - 1, left),
        device_id_type=MESH,
    )

    @pl.when(has_right)
    def _():
        below.start()

    @pl.when(has_left)
    def _():
        above.start()

    sends = []
    for i in sorted(range(1, bands), key=lambda i: -min(i, bands - i)):
        peer = lax.rem(band + i, bands)
        copy = pltpu.make_async_remote_copy(
            wide.at[:, pl.ds(pl.multiple_of(REACH + share * peer, REACH), share), :],
            mine.at[i],
            band_send.at[1, i],
            band_recv.at[1, i],
            device_id=(peer, shard),
            device_id_type=MESH,
        )
        copy.start()
        sends.append(copy)
    mine[0] = wide[:, pl.ds(pl.multiple_of(REACH + share * band, REACH), share), :]
    for i in range(1, bands):
        pltpu.make_async_copy(mix_in.at[i], mix_in.at[i], band_recv.at[0, i]).wait()
    for i in range(1, bands):
        pltpu.make_async_copy(mine.at[i], mine.at[i], band_recv.at[1, i]).wait()

    @pl.when(((band == 0) & has_left) | ((band == bands - 1) & has_right))
    def _():
        for i in range(bands):
            pltpu.make_async_copy(edge.at[i], edge.at[i], edge_recv.at[i]).wait()
        mine[...] += edge[...]

    for c in range(NCOMP):
        total = None
        for i in range(bands):
            for k in range(NBEAM):
                term = mix_in[i, c * NBEAM + k : c * NBEAM + k + 1, :] * mine[i, k]
                total = term if total is None else total + term
        out[c, 0] = total

    @pl.when(has_right)
    def _():
        to_right.wait_send()
        below.wait_send()

    @pl.when(has_left)
    def _():
        to_left.wait_send()
        above.wait_send()

    from_shards(meta_out, 1, peer_send.at[0])
    from_shards(vals_out, CAP, peer_send.at[1])
    for i in range(1, bands):
        pltpu.make_async_copy(mix_out, mix_out, band_send.at[0, i]).wait()
    for copy in sends:
        copy.wait_send()


def on_device(
    tod, filter_taps, det_weights, owner, tile_row, block_counts, beam_rows, beam_cols, mixing
):
    bands, shards = lax.axis_size("band"), lax.axis_size("tm")
    side = 8 if shards >= 16 else shards // 2
    det, samples = tod.shape[1:]
    slots = shards * CAP
    long = bands * REACH + 2 * REACH
    blocks = samples // PIX
    vmem = pl.BlockSpec(memory_space=pltpu.VMEM)
    return pl.pallas_call(
        functools.partial(kernel, bands, shards, side),
        out_shape=jax.ShapeDtypeStruct((NCOMP, 1, REACH, PIX), F32),
        in_specs=[pl.BlockSpec(memory_space=pltpu.HBM)] * 8
        + [pl.BlockSpec(memory_space=pltpu.SMEM)],
        out_specs=vmem,
        scratch_shapes=[
            pltpu.VMEM(filter_taps.shape, BF16),
            pltpu.VMEM((1, det), F32),
            pltpu.VMEM((1, blocks), jnp.int32),
            pltpu.VMEM((1, blocks), jnp.int32),
            pltpu.VMEM(beam_rows.shape, F32),
            pltpu.VMEM(beam_cols.shape, F32),
            pltpu.VMEM((1, NBEAM, NCOMP), F32),
            pltpu.VMEM((det, samples + 4 * HALF), BF16),
            pltpu.VMEM((2 * PIX + 16, LAGS * det), BF16),
            pltpu.VMEM((blocks + 3 * STEP, PIX), F32),
            pltpu.VMEM((blocks + 3 * STEP, PIX), F32),
            pltpu.VMEM((2 * PIX + 16, CHUNK), F32),
            pltpu.VMEM((2 * PIX + 16, CHUNK), F32),
            pltpu.VMEM((2, STEP, PIX), F32),
            pltpu.VMEM((2, STEP, PIX), F32),
            pltpu.VMEM((shards, PIX), F32),
            pltpu.VMEM((shards, PIX), F32),
            pltpu.VMEM((slots, PIX), F32),
            pltpu.VMEM((slots, PIX), F32),
            pltpu.VMEM((NCOMP * NBEAM, PIX), F32),
            pltpu.VMEM((bands, NCOMP * NBEAM, PIX), F32),
            pltpu.VMEM((NBEAM, long, PIX), F32),
            pltpu.VMEM((bands, NBEAM, REACH, PIX), F32),
            pltpu.VMEM((bands, NBEAM, REACH, PIX), F32),
            pltpu.SemaphoreType.DMA((PARTS,)),
            pltpu.SemaphoreType.DMA((7,)),
            pltpu.SemaphoreType.DMA((2,)),
            pltpu.SemaphoreType.DMA((2,)),
            pltpu.SemaphoreType.DMA((2,)),
            pltpu.SemaphoreType.DMA((2,)),
            pltpu.SemaphoreType.DMA((2, bands)),
            pltpu.SemaphoreType.DMA((2, bands)),
            pltpu.SemaphoreType.DMA((2,)),
            pltpu.SemaphoreType.DMA((bands,)),
        ],
        compiler_params=pltpu.CompilerParams(
            collective_id=0, has_side_effects=True, vmem_limit_bytes=50331648
        ),
    )(
        *(pltpu.with_memory_space_constraint(v, pltpu.HBM) for v in (tod,
        filter_taps,
        det_weights,
        owner.reshape(1, blocks),
        tile_row,
        beam_rows,
        beam_cols,
        mixing.transpose(1, 2, 0),)),
        block_counts,
    )


def solution(mesh):
    placed = (
        P("band", None, "tm"),
        P("band", None, None),
        P("band", None),
        P("band", "tm", None),
        P("band", "tm"),
        P("band", "tm"),
        P("band", None, None),
        P("band", None, None),
        P(None, "band", None),
    )
    return jax.shard_map(
        on_device,
        mesh=mesh,
        in_specs=placed,
        out_specs=P(None, "tm", "band", None),
        check_vma=False,
    )
```
